128 devices in a mesh: ha: 8 (over x_lo, y), wa: 16 (over x_hi, z, core).
Axes of the slice: x: 4 (x_hi: 2, x_lo: 2; x = x_hi * 2 + x_lo), y: 4, z: 4, core: 2. Of those that a mesh axis runs over, the one named last changes fastest.
Arguments:
- features: bfloat16 [4, 256, 512, 192], P(None, 'ha', 'wa'), may hold values from -6 to 6
- conv_first: bfloat16 [3, 3, 3, 192, 192], replicated, may hold values from -0.078125 to 0.078125
- bias_first: float32 [192], replicated, may hold values from -3 to 3
- gain_first: float32 [192], replicated, may hold values from 0.5 to 2
- conv_second: bfloat16 [3, 3, 3, 192, 192], replicated, may hold values from -0.078125 to 0.078125
- gain_second: float32 [192], replicated, may hold values from 0.5 to 2
- up_weight: bfloat16 [3, 3, 192, 96], replicated, may hold values from -0.15625 to 0.15625
- cotangent: bfloat16 [4, 512, 1024, 96], P(None, 'ha', 'wa'), may hold values from -6 to 6
Outputs:
- feature_grad: bfloat16 [4, 256, 512, 192], P(None, 'ha', 'wa')
The draws below stay inside these ranges and needn't reach their ends.
All inputs are finite; a program needn't handle non-finite values.
Results may differ from the reference program's by a relative error of at most 0.0051.
Values may be sent and summed in bfloat16 or wider, within the bound.
No kernel may reach another device: no remote copies, remote signals or barrier semaphores. Data moves between devices by JAX's collectives and lax.ppermute only.
A program may use at most 192 MiB of HBM per device.

```python
import math
import jax
import jax.numpy as jnp
from jax import lax

C = 192
C2 = 96
F = 4
H = 256
W = 512


def block_levels(rng, shape, shards, smallest, high):
    loudness = 1.0
    for dim, shards_of in shards:
        draws = jax.random.uniform(jax.random.fold_in(jax.random.fold_in(rng, 6), dim), (shards_of,), jnp.float32, smallest / len(shards), high / len(shards))
        loudness = loudness * jnp.repeat(jnp.exp(draws), shape[dim] // shards_of).reshape((-1,) + (1,) * (len(shape) - 1 - dim))
    return loudness


def noise(stream_key, dims, scale, reach, cuts=(), held_as=jnp.bfloat16):
    drawn = scale * jax.random.normal(stream_key, dims, jnp.float32)
    if cuts:
        drawn = drawn * block_levels(stream_key, dims, cuts, -0.22, 0.18)
    return jnp.clip(drawn, -reach, reach).astype(held_as)


def setup_inputs(seed: int = 0) -> dict:
    streams_of = jax.random.split(jax.random.key(seed), 9)
    features = noise(streams_of[0], (F, H, W, C), 1.0, 6.0, ((1, 8), (2, 16)))
    conv_first = noise(streams_of[1], (3, 3, 3, C, C), (27 * C) ** -0.5, 0.078125)
    bias_first = noise(streams_of[2], (C,), 0.5, 3.0, (), jnp.float32)
    gain_first = jnp.clip(jnp.exp(jax.random.uniform(streams_of[3], (C,), jnp.float32, math.log(0.5), math.log(2.0))), 0.5, 2.0)
    conv_second = noise(streams_of[4], (3, 3, 3, C, C), (27 * C) ** -0.5, 0.078125)
    gain_second = jnp.clip(jnp.exp(jax.random.uniform(streams_of[5], (C,), jnp.float32, math.log(0.5), math.log(2.0))), 0.5, 2.0)
    up_weight = noise(streams_of[6], (3, 3, C, C2), (9 * C) ** -0.5, 0.15625)
    cotangent = noise(streams_of[7], (F, 2 * H, 2 * W, C2), 1.0, 6.0, ((1, 8), (2, 16)))
    return {"features": features, "conv_first": conv_first, "bias_first": bias_first, "gain_first": gain_first, "conv_second": conv_second, "gain_second": gain_second, "up_weight": up_weight, "cotangent": cotangent}


def rms_scale(value):
    return lax.rsqrt(lax.optimization_barrier(jnp.mean(value * value, axis=-1, keepdims=True)) + 1e-06)

def silu_slope(value):
    sig = jax.nn.sigmoid(value)
    return sig * (1.0 + value * (1.0 - sig))

def rms_back(value, gain, grad):
    scale = rms_scale(value)
    scaled = gain * grad
    return scale * scaled - value * scale ** 3 * lax.optimization_barrier(jnp.mean(value * scaled, axis=-1, keepdims=True))

def causal_conv(field, weight, time_pads):
    return lax.conv_general_dilated(field[None].astype(jnp.float32), weight.astype(jnp.float32), (1, 1, 1), [time_pads, (1, 1), (1, 1)], dimension_numbers=('NDHWC', 'DHWIO', 'NDHWC'), precision=lax.Precision.HIGHEST)[0]

def reference(features, conv_first, bias_first, gain_first, conv_second, gain_second, up_weight, cotangent):
    frames, height, width, chans = features.shape
    feat_float = features.astype(jnp.float32)
    normed_first = feat_float * rms_scale(feat_float) * gain_first
    active_first = jax.nn.silu(normed_first).astype(jnp.bfloat16)
    pre_second = causal_conv(active_first, conv_first, (2, 0)) + bias_first
    normed_second = pre_second * rms_scale(pre_second) * gain_second
    up_flip = jnp.flip(up_weight, (0, 1)).swapaxes(2, 3)
    fine_grad = lax.conv_general_dilated(cotangent.astype(jnp.float32), up_flip.astype(jnp.float32), (1, 1), [(1, 1), (1, 1)], dimension_numbers=('NHWC', 'HWIO', 'NHWC'), precision=lax.Precision.HIGHEST)
    block_grad = fine_grad.reshape(frames, height, 2, width, 2, chans).sum(axis=(2, 4))
    block_low = block_grad.astype(jnp.bfloat16)
    second_flip = jnp.flip(conv_second, (0, 1, 2)).swapaxes(3, 4)
    second_grad = causal_conv(block_low, second_flip, (0, 2)) * silu_slope(normed_second)
    pre_grad = rms_back(pre_second, gain_second, second_grad).astype(jnp.bfloat16)
    first_flip = jnp.flip(conv_first, (0, 1, 2)).swapaxes(3, 4)
    first_grad = causal_conv(pre_grad, first_flip, (0, 2)) * silu_slope(normed_first)
    return (block_grad + rms_back(feat_float, gain_first, first_grad)).astype(jnp.bfloat16)
```

```python
import jax
import jax.numpy as jnp
from jax import lax
from jax.experimental import pallas as pl
from jax.experimental.pallas import tpu as pltpu
from jax.sharding import PartitionSpec as P

COLS = 40
WIDE = 48
F32 = jnp.float32
BF16 = jnp.bfloat16


def shift_pair(value_up, value_down, axis):
    count = lax.axis_size(axis)
    up = [(i, (i + 1) % count) for i in range(count - 1)]
    down = [(j, i) for i, j in up]
    return lax.ppermute(value_up, axis, up), lax.ppermute(value_down, axis, down)


def halves(field, axis):
    half = field.shape[-1] // 2
    return jnp.concatenate([field[..., :half], field[..., half:]], axis=axis)


def conv_weight(weight):
    packed = []
    for p in range(3):
        w = weight[:, p]
        part = [w[:, 0, :128], w[:, 1, :128], w[:, 2, :128], w[:, 0, 128:], w[:, 1, 128:]]
        if p == 0:
            part += [w[:, 2, 128:], weight[:, 1, 2, 128:]]
        if p == 2:
            part += [w[:, 2, 128:], jnp.zeros_like(w[:, 2, 128:])]
        packed += part
    return jnp.concatenate(packed, axis=1).reshape(3 * 1792, weight.shape[-1])


def up_taps(weight):
    w = jnp.flip(weight, (0, 1)).swapaxes(2, 3)
    return jnp.pad(w, ((0, 0), (0, 0), (0, 32), (0, 0))).reshape(1152, weight.shape[2])


def rms_scale(value):
    return lax.rsqrt(jnp.sum(value * value, axis=-1, keepdims=True) * (1.0 / 192) + 1e-06)


def sigmoid(value):
    return 1.0 / (1.0 + jnp.exp(-value))


def put_row(ref, t, e, value, count):
    low, high = value[:, :128], value[:, 128:]
    high = jnp.concatenate([high, high], axis=1)
    lane = lax.broadcasted_iota(jnp.int32, high.shape, 1)
    size = value.shape[0]
    high_next = pltpu.roll(high, size - 1, 0)[:count].astype(BF16)
    ref[t, e, :count, 0:128] = pltpu.roll(low, 1, 0)[:count].astype(BF16)
    ref[t, e, :count, 128:256] = low[:count].astype(BF16)
    ref[t, e, :count, 256:384] = pltpu.roll(low, size - 1, 0)[:count].astype(BF16)
    both = jnp.where(lane < 64, pltpu.roll(high, 1, 0), high)
    ref[t, e, :count, 384:512] = both[:count].astype(BF16)
    ref[t, e, :count, 512:576] = high_next[:, :64]
    ref[t, jnp.maximum(e - 1, 0), :count, 576:640] = high_next[:, 64:]


def conv_block(ref, w_ref, t, sign, row, rows):
    parts, lo, hi = [], 3, 0
    for k in range(3):
        s = t - 2 + k if sign > 0 else t + k
        if not 0 <= s <= 3:
            continue
        lo, hi = min(lo, k), max(hi, k + 1)
        for p, lanes in ((0, 640), (1, 512), (2, 640)):
            piece = ref[s, pl.ds(row + p, rows), :, 0:lanes]
            parts.append(piece.reshape(rows * piece.shape[1], lanes))
    lhs = jnp.concatenate(parts, axis=1)
    return jnp.dot(lhs, w_ref[lo * 1792 : hi * 1792, :], preferred_element_type=F32)


def body(
    flags, feat, before, after, feat_side, cot, cot_side, w1, w2t, w1t, wup, bias, gain1, gain2,
    out, act, grad, pre, block, acc, cot_wide, pooled, line,
):
    def columns(value):
        s = lax.broadcasted_iota(jnp.int32, value.shape, 0)
        good = (s < 32) | ((s < 34) & (flags[3] > 0)) | ((s >= 38) & (flags[2] > 0))
        return jnp.where(good, value, 0.0)

    def row_good(e, first, last):
        top = jnp.where(e < first, flags[0], 1)
        return jnp.where(e >= last, flags[1], top) > 0

    def activate(t, e, own):
        side = feat_side[t, e].astype(F32)
        x = jnp.concatenate([own.astype(F32), side], axis=0)
        n = x * rms_scale(x) * gain1[...]
        put_row(act, t, e, n * sigmoid(n), COLS)

    def edge_row(ref, t, r):
        return jnp.concatenate([ref[t, r, 0:32, :], ref[t, r, 32:64, :]], axis=1)

    def frame_active(t, carry):
        for r in range(2):
            activate(t, r, edge_row(before, t, r))

        def step(i, c):
            activate(t, i + 2, feat[t, i])
            return c

        lax.fori_loop(0, 32, step, 0)
        for r in range(2):
            activate(t, 34 + r, edge_row(after, t, r))
        act[t, 35, :, 576:640] = jnp.zeros((WIDE, 64), BF16)
        return carry

    lax.fori_loop(0, 4, frame_active, 0)

    for t in range(4):

        def first_conv(b, c):
            value = conv_block(act, w1, t, 1, b * 17, 17).reshape(17, WIDE, 192)
            pre[t, pl.ds(b * 17, 17)] = value[:, :COLS] + bias[...].reshape(1, 1, 192)
            return c

        lax.fori_loop(0, 2, first_conv, 0)

    line[...] = jnp.zeros_like(line)

    def frame_block(t, carry):
        def gather(f, row):
            cot_wide[f, 0:64, 0:96] = row
            cot_wide[f, 64:80, 0:96] = cot_side[t, f]

        for r in range(5):
            gather(r, before[t, 2 + r])
            gather(69 + r, after[t, 2 + r])

        def copy_row(y, c):
            gather(y + 5, cot[t, y])
            return c

        lax.fori_loop(0, 64, copy_row, 0)

        def pool(e, c):
            rows = [cot_wide[2 * e + m, :, 0:96].astype(F32) for m in range(3)]
            for m in range(2):
                line[m, :, 0:96] = rows[m] + rows[m + 1]
                even = line[m, pl.ds(0, 40, stride=2), :]
                odd = line[m, pl.ds(1, 40, stride=2), :]
                pooled[m, e, :COLS, 0:128] = (pltpu.roll(odd, 1, 0) + even).astype(BF16)
                pooled[m, e, :COLS, 128:256] = (even + odd).astype(BF16)
                pooled[m, e, :COLS, 256:384] = (odd + pltpu.roll(even, 39, 0)).astype(BF16)
            return c

        lax.fori_loop(0, 37, pool, 0)

        def up_conv(b, c):
            e0 = b * 12
            parts = [pooled[0, pl.ds(e0, 12)], pooled[1, pl.ds(e0, 12)], pooled[0, pl.ds(e0 + 1, 12)]]
            lhs = jnp.concatenate([x.reshape(12 * WIDE, 384) for x in parts], axis=1)
            acc[0:12] = jnp.dot(lhs, wup[...], preferred_element_type=F32).reshape(12, WIDE, 192)

            def store(r, c2):
                e = e0 + r
                value = acc[r, :COLS]
                value = jnp.where(row_good(e, 2, 34), columns(value), 0.0)
                put_row(grad, t, e, value, COLS)

                @pl.when((e >= 2) & (e < 34))
                def _():
                    block[t, e - 2] = value[:32]

                return c2

            lax.fori_loop(0, 12, store, 0)
            return c

        lax.fori_loop(0, 3, up_conv, 0)
        grad[t, 35, :, 576:640] = jnp.zeros((WIDE, 64), BF16)
        return carry

    lax.fori_loop(0, 4, frame_block, 0)

    for t in range(4):

        def second_conv(b, c):
            acc[0:17] = conv_block(grad, w2t, t, -1, b * 17, 17).reshape(17, WIDE, 192)

            def store(r, c2):
                o = b * 17 + r
                v = pre[t, o]
                scale = rms_scale(v)
                n = v * scale * gain2[...]
                s = sigmoid(n)
                u = gain2[...] * (acc[r, :COLS] * (s * (1.0 + n * (1.0 - s))))
                mean = jnp.sum(v * u, axis=-1, keepdims=True) * (1.0 / 192)
                g = scale * u - v * (scale * scale * scale * mean)
                g = jnp.where(row_good(o, 1, 33), columns(g), 0.0)
                put_row(act, t, o, g, 32)
                return c2

            lax.fori_loop(0, 17, store, 0)
            return c

        lax.fori_loop(0, 2, second_conv, 0)
        act[t, 33, :, 576:640] = jnp.zeros((WIDE, 64), BF16)

    for t in range(4):

        def last_conv(b, c):
            acc[0:16, 0:32] = conv_block(act.at[:, :, 0:32], w1t, t, -1, b * 16, 16).reshape(16, 32, 192)

            def store(r, c2):
                i = b * 16 + r
                x = feat[t, i].astype(F32)
                scale = rms_scale(x)
                n = x * scale * gain1[...]
                s = sigmoid(n)
                u = gain1[...] * (acc[r, 0:32] * (s * (1.0 + n * (1.0 - s))))
                mean = jnp.sum(x * u, axis=-1, keepdims=True) * (1.0 / 192)
                g = scale * u - x * (scale * scale * scale * mean)
                out[t, i] = (block[t, i] + g).astype(BF16)
                return c2

            lax.fori_loop(0, 16, store, 0)
            return c

        lax.fori_loop(0, 2, last_conv, 0)


def per_device(
    features, conv_first, bias_first, gain_first, conv_second, gain_second, up_weight, cotangent
):
    def rows(lo_f, lo_c):
        f = halves(features[:, lo_f : lo_f + 2], 2)
        return jnp.concatenate([f, cotangent[:, lo_c : lo_c + 5]], axis=1)

    before, after = shift_pair(rows(30, 59), rows(0, 0), "ha")

    def cols(lo_f, lo_c):
        f = [halves(features[:, :, lo_f : lo_f + 2], 1)]
        edge = []
        for r in (before, after):
            edge += [r[:, 0:2, lo_f : lo_f + 2], r[:, 0:2, 32 + lo_f : 34 + lo_f]]
        f = jnp.concatenate([edge[0], f[0][:, :32], edge[2], edge[1], f[0][:, 32:], edge[3]], axis=1)
        f = jnp.pad(f, ((0, 0), (0, 2), (0, 0), (0, 0)))
        c = [before[:, 2:, lo_c : lo_c + 5], cotangent[:, :, lo_c : lo_c + 5], after[:, 2:, lo_c : lo_c + 5]]
        return jnp.concatenate([jnp.concatenate(c, axis=1), f], axis=2)

    left, right = shift_pair(cols(30, 59), cols(0, 0), "wa")
    cot_side = jnp.concatenate(
        [right[:, :, :5], jnp.zeros(right.shape[:2] + (6, 96), BF16), left[:, :, :5]], axis=2
    )

    def feat_cols(side):
        return jnp.concatenate([side[:, :36, 5:], side[:, 36:72, 5:]], axis=3)

    feat_right, feat_left = feat_cols(right), feat_cols(left)
    gap = jnp.zeros(feat_right.shape[:2] + (4, 192), BF16)
    feat_side = jnp.concatenate([feat_right, gap, feat_left], axis=2)

    flip = lambda w: jnp.flip(w, (0, 1, 2)).swapaxes(3, 4)
    w1, w2t, w1t = conv_weight(conv_first), conv_weight(flip(conv_second)), conv_weight(flip(conv_first))
    ha, wa = lax.axis_index("ha"), lax.axis_index("wa")
    flags = jnp.stack(
        [ha > 0, ha < lax.axis_size("ha") - 1, wa > 0, wa < lax.axis_size("wa") - 1]
    ).astype(jnp.int32)
    vmem = pl.BlockSpec(memory_space=pltpu.VMEM)
    return pl.pallas_call(
        body,
        out_shape=jax.ShapeDtypeStruct(features.shape, BF16),
        in_specs=[pl.BlockSpec(memory_space=pltpu.SMEM)] + [vmem] * 13,
        out_specs=vmem,
        scratch_shapes=[
            pltpu.VMEM((4, 36, WIDE, 640), BF16),
            pltpu.VMEM((4, 36, WIDE, 640), BF16),
            pltpu.VMEM((4, 34, COLS, 192), F32),
            pltpu.VMEM((4, 32, 32, 192), F32),
            pltpu.VMEM((17, WIDE, 192), F32),
            pltpu.VMEM((76, 80, 128), BF16),
            pltpu.VMEM((2, 37, WIDE, 384), BF16),
            pltpu.VMEM((2, 80, 128), F32),
        ],
        compiler_params=pltpu.CompilerParams(vmem_limit_bytes=60 * 1024 * 1024),
        name="block_backward",
    )(
        flags, features, before, after, feat_side, cotangent, cot_side, w1, w2t, w1t,
        up_taps(up_weight), bias_first.reshape(1, 192), gain_first.reshape(1, 192),
        gain_second.reshape(1, 192),
    )


def solution(mesh):
    placed = (P(None, "ha", "wa", None), P(), P(), P(), P(), P(), P(), P(None, "ha", "wa", None))
    return jax.shard_map(
        per_device, mesh=mesh, in_specs=placed, out_specs=P(None, "ha", "wa", None), check_vma=False
    )
```

```python
import jax
import jax.numpy as jnp
from jax import lax
from jax.experimental import pallas as pl
from jax.experimental.pallas import tpu as pltpu
from jax.sharding import PartitionSpec as P

COLS = 40
WIDE = 48
LANES = (640, 512, 640)
F32 = jnp.float32
BF16 = jnp.bfloat16


def shift_pair(value_up, value_down, axis):
    count = lax.axis_size(axis)
    up = [(i, (i + 1) % count) for i in range(count - 1)]
    down = [(j, i) for i, j in up]
    return lax.ppermute(value_up, axis, up), lax.ppermute(value_down, axis, down)


def halves(field, axis):
    half = field.shape[-1] // 2
    return jnp.concatenate([field[..., :half], field[..., half:]], axis=axis)


def rms_scale(value):
    return lax.rsqrt(jnp.sum(value * value, axis=-1, keepdims=True) * (1.0 / 192) + 1e-06)


def sigmoid(value):
    return 0.5 * jnp.tanh(0.5 * value) + 0.5


def put_row(ref, e, value, count):
    low, high = value[:, :128], value[:, 128:]
    high = jnp.concatenate([high, high], axis=1)
    lane = lax.broadcasted_iota(jnp.int32, high.shape, 1)
    size = value.shape[0]
    high_next = pltpu.roll(high, size - 1, 0)[:count].astype(BF16)
    ref[e, :count, 0:128] = pltpu.roll(low, 1, 0)[:count].astype(BF16)
    ref[e, :count, 128:256] = low[:count].astype(BF16)
    ref[e, :count, 256:384] = pltpu.roll(low, size - 1, 0)[:count].astype(BF16)
    both = jnp.where(lane < 64, pltpu.roll(high, 1, 0), high)
    ref[e, :count, 384:512] = both[:count].astype(BF16)
    ref[e, :count, 512:576] = high_next[:, :64]
    before = e - 1 if isinstance(e, int) and e else jnp.maximum(e - 1, 0)
    ref[before, :count, 576:640] = high_next[:, 64:]


def weight_rows(w_ref, k):
    rows = []
    for p in range(3):
        w = [w_ref[k, p, q] for q in range(3)]
        rows += [w[0][:128], w[1][:128], w[2][:128], w[0][128:], w[1][128:]]
        if p == 0:
            rows += [w[2][128:], w_ref[k, 1, 2, 128:, :]]
        if p == 2:
            rows += [w[2][128:], jnp.zeros((64, 192), BF16)]
    return jnp.concatenate(rows, axis=0)


def pack_adjoint(dst, w_ref):
    for k in range(3):
        base = 0
        for p in range(3):
            w = [w_ref[2 - k, 2 - p, 2 - q] for q in range(3)]
            for q in range(3):
                dst[k, :, base + 128 * q : base + 128 * q + 128] = w[q][:, :128]
            dst[k, :, base + 384 : base + 512] = jnp.concatenate([w[0][:, 128:], w[1][:, 128:]], axis=1)
            if p != 1:
                other = w_ref[2 - k, 1, 0][:, 128:] if p == 0 else jnp.zeros((192, 64), BF16)
                dst[k, :, base + 512 : base + 640] = jnp.concatenate([w[2][:, 128:], other], axis=1)
            base += LANES[p]


def operand(refs, frames, row, rows, cols):
    parts = []
    for s in frames:
        for p in range(3):
            piece = refs[s][pl.ds(row + p, rows), :cols, 0 : LANES[p]]
            parts.append(piece.reshape(rows * cols, LANES[p]))
    return jnp.concatenate(parts, axis=1)


def body(*refs):
    flags, feat, feat_side, cot, cot_side, before, after, w1, w2, wup, bias, gain1, gain2, out = refs[:14]
    act, grad, pre, block = (refs[14 + 4 * n : 18 + 4 * n] for n in range(4))
    acc, pooled = refs[30:32], refs[32:34]
    line, mask, w2t, w1t, wu = refs[34:]

    for n in range(4):
        act[n][35, :, 576:640] = jnp.zeros((WIDE, 64), BF16)
        grad[n][35, :, 576:640] = jnp.zeros((WIDE, 64), BF16)
    line[...] = jnp.zeros_like(line)
    s = lax.broadcasted_iota(jnp.int32, mask.shape, 0)
    good = (s < 32) | ((s < 34) & (flags[3] > 0)) | ((s >= 38) & (flags[2] > 0))
    mask[...] = jnp.where(good, 1.0, 0.0)
    pack_adjoint(w2t, w2)
    pack_adjoint(w1t, w1)
    for p in range(3):
        for q in range(3):
            tap = 128 * (3 * p + q)
            wu[:, tap : tap + 96] = wup[2 - p, 2 - q]
            wu[:, tap + 96 : tap + 128] = jnp.zeros((192, 32), BF16)

    def edge(value, b, r, first, last):
        if r in first:
            return value * jnp.where((b == 0) & (flags[0] == 0), 0.0, 1.0)
        if r in last:
            return value * jnp.where((b == 1) & (flags[1] == 0), 0.0, 1.0)
        return value

    def activate(t):
        def one(e, x):
            x = x.astype(F32)
            n = x * rms_scale(x) * gain1[...]
            put_row(act[t], e, n * sigmoid(n), COLS)

        def run(b):
            for r in range(2):
                x = jnp.where(b == 0, before[t, r].astype(F32), after[t, r].astype(F32))
                one(r + 34 * b, jnp.concatenate([x[:COLS], x[COLS:]], axis=1))
            for r in range(16):
                i = 16 * b + r
                one(i + 2, jnp.concatenate([feat[t, i].astype(F32), feat_side[t, i].astype(F32)], axis=0))

        return run

    def pool(t):
        dst = pooled[t % 2]

        def own(y):
            return jnp.concatenate([cot[t, y], cot_side[t, y]], axis=0).astype(F32)

        def one(e, rows, slot):
            for m in range(2):
                line[slot, m, :, 0:96] = rows[m] + rows[m + 1]
                even = line[slot, m, pl.ds(0, 40, stride=2), :]
                odd = line[slot, m, pl.ds(1, 40, stride=2), :]
                dst[m, e, :COLS, 0:128] = (pltpu.roll(odd, 1, 0) + even).astype(BF16)
                dst[m, e, :COLS, 128:256] = (even + odd).astype(BF16)
                dst[m, e, :COLS, 256:384] = (odd + pltpu.roll(even, 39, 0)).astype(BF16)

        def run(b):
            top = [before[t, 2 + r].astype(F32) for r in range(5)] + [own(0), own(1)]
            low = [own(63)] + [after[t, 2 + r].astype(F32) for r in range(5)]
            low.append(low[-1])
            ends = [jnp.where(b == 0, x, y) for x, y in zip(top, low)]
            for r in range(3):
                one(34 * b + r, ends[2 * r : 2 * r + 3], r)
            for r in range(16):
                e = jnp.minimum(3 + 16 * b + r, 33)
                one(e, [own(2 * e - 5 + m) for m in range(3)], 3 + r % 13)

        return run

    def keep_block(t):
        def run(b):
            for r in range(18):
                e = 18 * b + r
                value = edge(acc[t % 2][e, :COLS] * mask[...], b, r, (0, 1), (16, 17))
                put_row(grad[t], e, value, COLS)
                block[t][e] = value[:32]

        return run

    def norm_back(v, gain, top):
        scale = rms_scale(v)
        n = v * scale * gain
        s = sigmoid(n)
        u = gain * (top * (s * (1.0 + n * (1.0 - s))))
        mean = jnp.sum(v * u, axis=-1, keepdims=True) * (1.0 / 192)
        return scale * u - v * (scale * scale * scale * mean)

    def pre_grad(t):
        def run(b):
            for r in range(17):
                o = 17 * b + r
                g = norm_back(pre[t][o], gain2[...], acc[t % 2][o, :COLS])
                put_row(act[t], o, edge(g * mask[...], b, r, (0,), (16,)), 32)

        return run

    def finish(t):
        def run(b):
            for r in range(16):
                i = 16 * b + r
                g = norm_back(feat[t, i].astype(F32), gain1[...], acc[t % 2][i, 0:32])
                out[t, i] = (block[t][i + 2] + g).astype(BF16)

        return run

    def first_conv(t):
        frames = range(max(0, t - 2), t + 1)

        def run(b):
            w = jnp.concatenate([weight_rows(w1, s - t + 2) for s in frames], axis=0)
            value = jnp.dot(operand(act, frames, 17 * b, 17, WIDE), w, preferred_element_type=F32)
            pre[t][pl.ds(17 * b, 17)] = value.reshape(17, WIDE, 192)[:, :COLS] + bias[...].reshape(1, 1, 192)

        return run

    def adjoint(src, w, t, rows, cols):
        frames = range(t, min(4, t + 3))

        def run(b):
            rhs = jnp.concatenate([w[s - t] for s in frames], axis=1)
            lhs = operand(src, frames, rows * b, rows, cols)
            value = lax.dot_general(lhs, rhs, (((1,), (1,)), ((), ())), preferred_element_type=F32)
            acc[t % 2][pl.ds(rows * b, rows), :cols] = value.reshape(rows, cols, 192)

        return run

    def up_conv(t):
        src = pooled[t % 2]

        def run(b):
            parts = [src[0, pl.ds(18 * b, 18)], src[1, pl.ds(18 * b, 18)], src[0, pl.ds(18 * b + 1, 18)]]
            lhs = jnp.concatenate([x.reshape(18 * WIDE, 384) for x in parts], axis=1)
            value = lax.dot_general(lhs, wu[...], (((1,), (1,)), ((), ())), preferred_element_type=F32)
            acc[t % 2][pl.ds(18 * b, 18)] = value.reshape(18, WIDE, 192)

        return run

    second = lambda t: adjoint(grad, w2t, t, 17, WIDE)
    last = lambda t: adjoint(act, w1t, t, 16, 32)
    steps = [
        [activate(0)],
        [first_conv(0), activate(1)],
        [first_conv(1), activate(2)],
        [first_conv(2), activate(3)],
        [first_conv(3), pool(0)],
        [up_conv(0), pool(1)],
        [up_conv(1), keep_block(0), pool(2)],
        [up_conv(2), keep_block(1), pool(3)],
        [up_conv(3), keep_block(2)],
        [second(0), keep_block(3)],
        [second(1), pre_grad(0)],
        [second(2), pre_grad(1)],
        [second(3), pre_grad(2)],
        [last(0), pre_grad(3)],
        [last(1), finish(0)],
        [last(2), finish(1)],
        [last(3), finish(2)],
        [finish(3)],
    ]
    for jobs in steps:

        def step(b, carry):
            for job in jobs:
                job(b)
            return carry

        lax.fori_loop(0, 2, step, 0)


def per_device(
    features, conv_first, bias_first, gain_first, conv_second, gain_second, up_weight, cotangent
):
    def cols(lo_f, lo_c):
        parts = [cotangent[:, :, lo_c : lo_c + 5], halves(features[:, :, lo_f : lo_f + 2], 1)]
        return jnp.pad(jnp.concatenate(parts, axis=2), ((0, 0), (0, 0), (0, 1), (0, 0)))

    left, right = shift_pair(cols(30, 59), cols(0, 0), "wa")

    def ring(first, last, width):
        gap = jnp.zeros(first.shape[:2] + (width - 2 * first.shape[2], first.shape[3]), BF16)
        return jnp.concatenate([first, gap, last], axis=2)

    cot_side = ring(right[:, :, :5], left[:, :, :5], 16)
    whole = lambda side: jnp.concatenate([side[:, :32, 5:7], side[:, 32:, 5:7]], axis=3)
    feat_side = ring(whole(right), whole(left), 8)

    def rows(lo_f, lo_c):
        f = jnp.concatenate([features[:, lo_f : lo_f + 2], feat_side[:, lo_f : lo_f + 2]], axis=2)
        c = jnp.concatenate([cotangent[:, lo_c : lo_c + 5], cot_side[:, lo_c : lo_c + 5]], axis=2)
        return jnp.concatenate([halves(f, 2), c], axis=1)

    before, after = shift_pair(rows(30, 59), rows(0, 0), "ha")
    ha, wa = lax.axis_index("ha"), lax.axis_index("wa")
    flags = jnp.stack(
        [ha > 0, ha < lax.axis_size("ha") - 1, wa > 0, wa < lax.axis_size("wa") - 1]
    ).astype(jnp.int32)
    vmem = pl.BlockSpec(memory_space=pltpu.VMEM)
    return pl.pallas_call(
        body,
        out_shape=jax.ShapeDtypeStruct(features.shape, BF16),
        in_specs=[pl.BlockSpec(memory_space=pltpu.SMEM)] + [vmem] * 12,
        out_specs=vmem,
        scratch_shapes=[pltpu.VMEM((36, WIDE, 640), BF16)] * 8
        + [pltpu.VMEM((34, COLS, 192), F32)] * 4
        + [pltpu.VMEM((36, 32, 192), F32)] * 4
        + [pltpu.VMEM((36, WIDE, 192), F32)] * 2
        + [pltpu.VMEM((2, 37, WIDE, 384), BF16)] * 2
        + [
            pltpu.VMEM((16, 2, 80, 128), F32),
            pltpu.VMEM((COLS, 192), F32),
            pltpu.VMEM((3, 192, 1792), BF16),
            pltpu.VMEM((3, 192, 1792), BF16),
            pltpu.VMEM((192, 1152), BF16),
        ],
        compiler_params=pltpu.CompilerParams(vmem_limit_bytes=60 * 1024 * 1024),
        name="block_backward",
    )(
        flags, features, feat_side, cotangent, cot_side, before, after, conv_first, conv_second,
        up_weight, bias_first.reshape(1, 192), gain_first.reshape(1, 192), gain_second.reshape(1, 192),
    )


def solution(mesh):
    placed = (P(None, "ha", "wa", None), P(), P(), P(), P(), P(), P(), P(None, "ha", "wa", None))
    return jax.shard_map(
        per_device, mesh=mesh, in_specs=placed, out_specs=P(None, "ha", "wa", None), check_vma=False
    )
```

```python
import jax
import jax.numpy as jnp
from jax import lax
from jax.experimental import pallas as pl
from jax.experimental.pallas import tpu as pltpu
from jax.sharding import PartitionSpec as P

COLS = 40
WIDE = 48
DEEP = 5
LANES = (640, 512, 640)
F32 = jnp.float32
BF16 = jnp.bfloat16


def shift_pair(value_up, value_down, axis):
    count = lax.axis_size(axis)
    up = [(i, (i + 1) % count) for i in range(count - 1)]
    down = [(j, i) for i, j in up]
    return lax.ppermute(value_up, axis, up), lax.ppermute(value_down, axis, down)


def halves(field, axis):
    half = field.shape[-1] // 2
    return jnp.concatenate([field[..., :half], field[..., half:]], axis=axis)


def rms_scale(value):
    return lax.rsqrt(jnp.sum(value * value, axis=-1, keepdims=True) * (1.0 / 192) + 1e-06)


def sigmoid(value):
    return 0.5 * jnp.tanh(0.5 * value) + 0.5


def put_row(ref, tail, e, value):
    low, high = value[:, :128], value[:, 128:]
    high = jnp.concatenate([high, high], axis=1)
    lane = lax.broadcasted_iota(jnp.int32, high.shape, 1)
    left = jnp.where(lane < 64, pltpu.roll(high, 1, 0), high)
    after = pltpu.roll(high, COLS - 1, 0)
    before = jnp.maximum(e - 1, 0)
    for n, x in enumerate([pltpu.roll(low, 1, 0), low, pltpu.roll(low, COLS - 1, 0), left]):
        ref[e, :, 128 * n : 128 * n + 128] = x[:32].astype(BF16)
        if tail is not None:
            tail[n, pl.ds(8 * e, 8), :] = x[32:]
    own = after[:32].astype(BF16)
    ref[e, :, 512:576] = own[:, :64]
    ref[before, :, 576:640] = own[:, 64:]
    if tail is not None:
        tail[4, pl.ds(8 * e, 8), 0:64] = after[32:, :64]
        tail[4, pl.ds(8 * before, 8), 64:128] = after[32:, 64:]


def build_strip(dst, tail):
    for r in range(DEEP + 2):
        for n in range(5):
            sides = [tail[n, pl.ds(8 * r + first, 8, stride=8 * DEEP), :] for first in (7, 0)]
            dst[r, :, 128 * n : 128 * n + 128] = jnp.concatenate(sides, axis=0).astype(BF16)


def weight_rows(w_ref, k):
    rows = []
    for p in range(3):
        w = [w_ref[k, p, q] for q in range(3)]
        rows += [w[0][:128], w[1][:128], w[2][:128], w[0][128:], w[1][128:]]
        if p == 0:
            rows += [w[2][128:], w_ref[k, 1, 2, 128:, :]]
        if p == 2:
            rows += [w[2][128:], jnp.zeros((64, 192), BF16)]
    return jnp.concatenate(rows, axis=0)


def pack_adjoint(dst, w_ref):
    for k in range(3):
        base = 0
        for p in range(3):
            w = [w_ref[2 - k, 2 - p, 2 - q] for q in range(3)]
            for q in range(3):
                dst[k, :, base + 128 * q : base + 128 * q + 128] = w[q][:, :128]
            dst[k, :, base + 384 : base + 512] = jnp.concatenate([w[0][:, 128:], w[1][:, 128:]], axis=1)
            if p != 1:
                other = w_ref[2 - k, 1, 0][:, 128:] if p == 0 else jnp.zeros((192, 64), BF16)
                dst[k, :, base + 512 : base + 640] = jnp.concatenate([w[2][:, 128:], other], axis=1)
            base += LANES[p]


def operand(refs, strips, frames, row, rows, strip_row):
    parts = []
    for s in frames:
        for p in range(3):
            lanes = LANES[p]
            piece = refs[s][pl.ds(row + p, rows), :, 0:lanes].reshape(rows * 32, lanes)
            if strips is not None:
                side = strips[s][pl.ds(strip_row + p, 3), :, 0:lanes].reshape(48, lanes)
                piece = jnp.concatenate([piece, side], axis=0)
            parts.append(piece)
    return jnp.concatenate(parts, axis=1)


def body(*refs):
    flags, feat, feat_side, cot, cot_side, before, after, w1, w2, wup, bias, gain1, gain2, out = refs[:14]
    act, grad, act_strip, grad_strip, pre, pre_strip, block = (refs[14 + 4 * n : 18 + 4 * n] for n in range(7))
    acc_up, acc, acc_strip, pooled = (refs[42 + 2 * n : 44 + 2 * n] for n in range(4))
    acc_last = (refs[50], acc_up[1], acc_up[0], refs[50])
    act_tail, grad_tail, edges, line, mask, strip_mask, w2t, w1t, wu = refs[51:]

    for n in range(4):
        act[n][35, :, 576:640] = jnp.zeros((32, 64), BF16)
        grad[n][35, :, 576:640] = jnp.zeros((32, 64), BF16)
    for tail in (act_tail, grad_tail):
        tail[:, 35 * 8 :, :] = jnp.zeros((5, 56, 128), F32)
    line[...] = jnp.zeros_like(line)
    s = lax.broadcasted_iota(jnp.int32, mask.shape, 0)
    good = (s < 32) | ((s < 34) & (flags[3] > 0)) | ((s >= 38) & (flags[2] > 0))
    mask[...] = jnp.where(good, 1.0, 0.0)
    r, s = (lax.broadcasted_iota(jnp.int32, strip_mask.shape, n) for n in range(2))
    o = DEEP * lax.rem(s, 8) + r
    good = jnp.where(s < 8, flags[2], flags[3]) > 0
    good &= ((o > 0) | (flags[0] > 0)) & ((o < 33) | (flags[1] > 0))
    strip_mask[...] = jnp.where(good, 1.0, 0.0)
    pack_adjoint(w2t, w2)
    pack_adjoint(w1t, w1)
    for p in range(3):
        for q in range(3):
            tap = 128 * (3 * p + q)
            wu[:, tap : tap + 96] = wup[2 - p, 2 - q]
            wu[:, tap + 96 : tap + 128] = jnp.zeros((192, 32), BF16)

    def edge(value, b, r, first, last):
        if r in first:
            return value * jnp.where((b == 0) & (flags[0] == 0), 0.0, 1.0)
        if r in last:
            return value * jnp.where((b == 1) & (flags[1] == 0), 0.0, 1.0)
        return value

    def activate(t):
        def one(e, x):
            x = x.astype(F32)
            n = x * rms_scale(x) * gain1[...]
            put_row(act[t], act_tail, e, n * sigmoid(n))

        def run(b):
            for r in range(2):
                x = jnp.where(b == 0, before[t, r].astype(F32), after[t, r].astype(F32))
                one(r + 34 * b, jnp.concatenate([x[:COLS], x[COLS:]], axis=1))
            for r in range(16):
                i = 16 * b + r
                one(i + 2, jnp.concatenate([feat[t, i].astype(F32), feat_side[t, i].astype(F32)], axis=0))

        return run

    def pool(t):
        dst = pooled[t % 2]

        def own(y):
            return jnp.concatenate([cot[t, y], cot_side[t, y]], axis=0).astype(F32)

        def one(e, rows, slot):
            for m in range(2):
                line[slot, m, :, 0:96] = rows[m] + rows[m + 1]
                even = line[slot, m, pl.ds(0, 40, stride=2), :]
                odd = line[slot, m, pl.ds(1, 40, stride=2), :]
                dst[m, e, :COLS, 0:128] = (pltpu.roll(odd, 1, 0) + even).astype(BF16)
                dst[m, e, :COLS, 128:256] = (even + odd).astype(BF16)
                dst[m, e, :COLS, 256:384] = (odd + pltpu.roll(even, 39, 0)).astype(BF16)

        def run(b):
            top = [before[t, 2 + r].astype(F32) for r in range(5)] + [own(0), own(1)]
            low = [own(63)] + [after[t, 2 + r].astype(F32) for r in range(5)]
            low.append(low[-1])
            ends = [jnp.where(b == 0, x, y) for x, y in zip(top, low)]
            for r in range(3):
                one(34 * b + r, ends[2 * r : 2 * r + 3], r)
            for r in range(16):
                e = jnp.minimum(3 + 16 * b + r, 33)
                one(e, [own(2 * e - 5 + m) for m in range(3)], 3 + r % 13)

        return run

    def keep_block(t):
        def run(b):
            for r in range(18):
                e = 18 * b + r
                value = edge(acc_up[t % 2][e] * mask[...], b, r, (0, 1), (16, 17))
                put_row(grad[t], grad_tail, e, value)
                block[t][e] = value[:32]

        return run

    def norm_back(v, gain, top):
        scale = rms_scale(v)
        n = v * scale * gain
        s = sigmoid(n)
        u = gain * (top * (s * (1.0 + n * (1.0 - s))))
        mean = jnp.sum(v * u, axis=-1, keepdims=True) * (1.0 / 192)
        return scale * u - v * (scale * scale * scale * mean)

    def strip_grad(t):
        g = norm_back(pre_strip[t][...], gain2[...].reshape(1, 1, 192), acc_strip[t % 2][...])
        g = g * strip_mask[...]
        for r in range(DEEP):
            edges[16 * r : 16 * r + 16, :] = g[r]

    def pre_grad(t):
        spot = lax.broadcasted_iota(jnp.int32, (8, 192), 0)

        def run(b):
            for r in range(17):
                o = 17 * b + r
                g = norm_back(pre[t][o], gain2[...], acc[t % 2][o])
                at = 16 * lax.rem(o, DEEP) + lax.div(o, DEEP)
                left, right = edges[pl.ds(at, 1), :], edges[pl.ds(at + 8, 1), :]
                side = jnp.where(spot == 0, right, jnp.where(spot == 7, left, 0.0))
                put_row(act[t], None, o, jnp.concatenate([edge(g, b, r, (0,), (16,)), side], axis=0))

        return run

    def finish(t):
        def run(b):
            for r in range(16):
                i = 16 * b + r
                g = norm_back(feat[t, i].astype(F32), gain1[...], acc_last[t][i, :32])
                out[t, i] = (block[t][i + 2] + g).astype(BF16)

        return run

    def split(value, b, main, strip, add):
        main[pl.ds(17 * b, 17)] = value[: 17 * 32].reshape(17, 32, 192) + add
        strip[pl.ds(2 * b, 3)] = value[17 * 32 :].reshape(3, 16, 192) + add

    def first_conv(t):
        frames = range(max(0, t - 2), t + 1)

        def run(b):
            w = jnp.concatenate([weight_rows(w1, s - t + 2) for s in frames], axis=0)
            lhs = operand(act, act_strip, frames, 17 * b, 17, 2 * b)
            value = jnp.dot(lhs, w, preferred_element_type=F32)
            split(value, b, pre[t], pre_strip[t], bias[...].reshape(1, 1, 192))

        return run

    def transposed(lhs, w, frames):
        rhs = jnp.concatenate([w[s - frames[0]] for s in frames], axis=1)
        return lax.dot_general(lhs, rhs, (((1,), (1,)), ((), ())), preferred_element_type=F32)

    def second(t):
        frames = range(t, min(4, t + 3))

        def run(b):
            value = transposed(operand(grad, grad_strip, frames, 17 * b, 17, 2 * b), w2t, frames)
            split(value, b, acc[t % 2], acc_strip[t % 2], 0.0)

        return run

    def last(t):
        frames = range(t, min(4, t + 3))

        def run(b):
            value = transposed(operand(act, None, frames, 16 * b, 16, 0), w1t, frames)
            acc_last[t][pl.ds(16 * b, 16), :32] = value.reshape(16, 32, 192)

        return run

    def up_conv(t):
        src = pooled[t % 2]

        def run(b):
            parts = [src[0, pl.ds(18 * b, 18)], src[1, pl.ds(18 * b, 18)], src[0, pl.ds(18 * b + 1, 18)]]
            lhs = jnp.concatenate([x.reshape(18 * WIDE, 384) for x in parts], axis=1)
            value = lax.dot_general(lhs, wu[...], (((1,), (1,)), ((), ())), preferred_element_type=F32)
            acc_up[t % 2][pl.ds(18 * b, 18)] = value.reshape(18, WIDE, 192)[:, :COLS]

        return run

    act_done = lambda t: lambda: build_strip(act_strip[t], act_tail)
    grad_done = lambda t: lambda: build_strip(grad_strip[t], grad_tail)
    second_done = lambda t: lambda: strip_grad(t)
    steps = [
        ([activate(0), pool(3)], [act_done(0)]),
        ([first_conv(0), up_conv(3), activate(1), pool(2)], [act_done(1)]),
        ([first_conv(1), up_conv(2), activate(2), keep_block(3)], [act_done(2), grad_done(3)]),
        ([first_conv(2), activate(3), keep_block(2)], [act_done(3), grad_done(2)]),
        ([first_conv(3), second(3), pool(1), pool(0)], [second_done(3)]),
        ([second(2), up_conv(1), pre_grad(3)], [second_done(2)]),
        ([up_conv(0), last(3), keep_block(1), pre_grad(2)], [grad_done(1)]),
        ([second(1), keep_block(0), finish(3)], [grad_done(0), second_done(1)]),
        ([second(0), pre_grad(1)], [second_done(0)]),
        ([last(2), last(1), pre_grad(0)], []),
        ([last(0), finish(2), finish(1)], []),
        ([finish(0)], []),
    ]
    for jobs, then in steps:

        def step(b, carry):
            for job in jobs:
                job(b)
            return carry

        lax.fori_loop(0, 2, step, 0)
        for job in then:
            job()


def per_device(
    features, conv_first, bias_first, gain_first, conv_second, gain_second, up_weight, cotangent
):
    def cols(lo_f, lo_c):
        parts = [cotangent[:, :, lo_c : lo_c + 5], halves(features[:, :, lo_f : lo_f + 2], 1)]
        return jnp.pad(jnp.concatenate(parts, axis=2), ((0, 0), (0, 0), (0, 1), (0, 0)))

    left, right = shift_pair(cols(30, 59), cols(0, 0), "wa")

    def ring(first, last, width):
        gap = jnp.zeros(first.shape[:2] + (width - 2 * first.shape[2], first.shape[3]), BF16)
        return jnp.concatenate([first, gap, last], axis=2)

    cot_side = ring(right[:, :, :5], left[:, :, :5], 16)
    whole = lambda side: jnp.concatenate([side[:, :32, 5:7], side[:, 32:, 5:7]], axis=3)
    feat_side = ring(whole(right), whole(left), 8)

    def rows(lo_f, lo_c):
        f = jnp.concatenate([features[:, lo_f : lo_f + 2], feat_side[:, lo_f : lo_f + 2]], axis=2)
        c = jnp.concatenate([cotangent[:, lo_c : lo_c + 5], cot_side[:, lo_c : lo_c + 5]], axis=2)
        return jnp.concatenate([halves(f, 2), c], axis=1)

    before, after = shift_pair(rows(30, 59), rows(0, 0), "ha")
    ha, wa = lax.axis_index("ha"), lax.axis_index("wa")
    flags = jnp.stack(
        [ha > 0, ha < lax.axis_size("ha") - 1, wa > 0, wa < lax.axis_size("wa") - 1]
    ).astype(jnp.int32)
    vmem = pl.BlockSpec(memory_space=pltpu.VMEM)
    return pl.pallas_call(
        body,
        out_shape=jax.ShapeDtypeStruct(features.shape, BF16),
        in_specs=[pl.BlockSpec(memory_space=pltpu.SMEM)] + [vmem] * 12,
        out_specs=vmem,
        scratch_shapes=[pltpu.VMEM((36, 32, 640), BF16)] * 8
        + [pltpu.VMEM((DEEP + 2, 16, 640), BF16)] * 8
        + [pltpu.VMEM((34, 32, 192), F32)] * 4
        + [pltpu.VMEM((DEEP, 16, 192), F32)] * 4
        + [pltpu.VMEM((36, 32, 192), F32)] * 4
        + [pltpu.VMEM((36, COLS, 192), F32)] * 2
        + [pltpu.VMEM((34, 32, 192), F32)] * 2
        + [pltpu.VMEM((DEEP, 16, 192), F32)] * 2
        + [pltpu.VMEM((2, 37, WIDE, 384), BF16)] * 2
        + [pltpu.VMEM((32, 32, 192), F32)]
        + [pltpu.VMEM((5, 8 * (7 + 7 * DEEP), 128), F32)] * 2
        + [
            pltpu.VMEM((16 * DEEP, 192), F32),
            pltpu.VMEM((16, 2, 80, 128), F32),
            pltpu.VMEM((COLS, 192), F32),
            pltpu.VMEM((DEEP, 16, 192), F32),
            pltpu.VMEM((3, 192, 1792), BF16),
            pltpu.VMEM((3, 192, 1792), BF16),
            pltpu.VMEM((192, 1152), BF16),
        ],
        compiler_params=pltpu.CompilerParams(vmem_limit_bytes=60 * 1024 * 1024),
        name="block_backward",
    )(
        flags, features, feat_side, cotangent, cot_side, before, after, conv_first, conv_second,
        up_weight, bias_first.reshape(1, 192), gain_first.reshape(1, 192), gain_second.reshape(1, 192),
    )


def solution(mesh):
    placed = (P(None, "ha", "wa", None), P(), P(), P(), P(), P(), P(), P(None, "ha", "wa", None))
    return jax.shard_map(
        per_device, mesh=mesh, in_specs=placed, out_specs=P(None, "ha", "wa", None), check_vma=False
    )
```

```python
import jax
import jax.numpy as jnp
from jax import lax
from jax.experimental import pallas as pl
from jax.experimental.pallas import tpu as pltpu
from jax.sharding import PartitionSpec as P

COLS = 40
WIDE = 48
DEEP = 5
LANES = (640, 512, 640)
F32 = jnp.float32
BF16 = jnp.bfloat16


def shift_pair(value_up, value_down, axis):
    count = lax.axis_size(axis)
    up = [(i, (i + 1) % count) for i in range(count - 1)]
    down = [(j, i) for i, j in up]
    return lax.ppermute(value_up, axis, up), lax.ppermute(value_down, axis, down)


def rms_scale(value):
    return lax.rsqrt(jnp.sum(value * value, axis=-1, keepdims=True) * (1.0 / 192) + 1e-06)


def sigmoid(value):
    return 0.5 * jnp.tanh(0.5 * value) + 0.5


def put_row(ref, tail, e, value):
    low, high = value[:, :128], value[:, 128:]
    high = jnp.concatenate([high, high], axis=1)
    lane = lax.broadcasted_iota(jnp.int32, high.shape, 1)
    left = jnp.where(lane < 64, pltpu.roll(high, 1, 0), high)
    after = pltpu.roll(high, COLS - 1, 0)
    before = jnp.maximum(e - 1, 0)
    for n, x in enumerate([pltpu.roll(low, 1, 0), low, pltpu.roll(low, COLS - 1, 0), left]):
        ref[e, :, 128 * n : 128 * n + 128] = x[:32].astype(BF16)
        if tail is not None:
            tail[n, pl.ds(8 * e, 8), :] = x[32:]
    own = after[:32].astype(BF16)
    ref[e, :, 512:576] = own[:, :64]
    ref[before, :, 576:640] = own[:, 64:]
    if tail is not None:
        tail[4, pl.ds(8 * e, 8), 0:64] = after[32:, :64]
        tail[4, pl.ds(8 * before, 8), 64:128] = after[32:, 64:]


def build_strip(dst, tail):
    for r in range(DEEP + 2):
        for n in range(5):
            sides = [tail[n, pl.ds(8 * r + first, 8, stride=8 * DEEP), :] for first in (7, 0)]
            dst[r, :, 128 * n : 128 * n + 128] = jnp.concatenate(sides, axis=0).astype(BF16)


def weight_rows(w_ref, k):
    rows = []
    for p in range(3):
        w = [w_ref[k, p, q] for q in range(3)]
        rows += [w[0][:128], w[1][:128], w[2][:128], w[0][128:], w[1][128:]]
        if p == 0:
            rows += [w[2][128:], w_ref[k, 1, 2, 128:, :]]
        if p == 2:
            rows += [w[2][128:], jnp.zeros((64, 192), BF16)]
    return jnp.concatenate(rows, axis=0)


def pack_adjoint(dst, w_ref):
    for k in range(3):
        base = 0
        for p in range(3):
            w = [w_ref[2 - k, 2 - p, 2 - q] for q in range(3)]
            for q in range(3):
                dst[k, :, base + 128 * q : base + 128 * q + 128] = w[q][:, :128]
            dst[k, :, base + 384 : base + 512] = jnp.concatenate([w[0][:, 128:], w[1][:, 128:]], axis=1)
            if p != 1:
                other = w_ref[2 - k, 1, 0][:, 128:] if p == 0 else jnp.zeros((192, 64), BF16)
                dst[k, :, base + 512 : base + 640] = jnp.concatenate([w[2][:, 128:], other], axis=1)
            base += LANES[p]


def operand(refs, strips, frames, row, rows, strip_row):
    parts = []
    for s in frames:
        for p in range(3):
            lanes = LANES[p]
            piece = refs[s][pl.ds(row + p, rows), :, 0:lanes].reshape(rows * 32, lanes)
            if strips is not None:
                side = strips[s][pl.ds(strip_row + p, 3), :, 0:lanes].reshape(48, lanes)
                piece = jnp.concatenate([piece, side], axis=0)
            parts.append(piece)
    return jnp.concatenate(parts, axis=1)


def conv_dot(lhs, w, axis):
    return lax.dot_general(lhs, w, (((1,), (axis,)), ((), ())), preferred_element_type=F32)


def split(value, b, main, strip, add):
    main[pl.ds(17 * b, 17)] = value[: 17 * 32].reshape(17, 32, 192) + add
    strip[pl.ds(2 * b, 3)] = value[17 * 32 :].reshape(3, 16, 192) + add


def run_steps(steps):
    for jobs, then in steps:

        def step(b, carry):
            for job in jobs:
                job(b)
            return carry

        lax.fori_loop(0, 2, step, 0)
        for job in then:
            job()


def forward(*refs):
    feat, feat_side, before, after, w1, bias, gain1, pre, pre_strip = refs[:9]
    act, act_strip = refs[9:13], refs[13:17]
    act_tail, act_rows = refs[17:]
    for n in range(4):
        act[n][35, :, 576:640] = jnp.zeros((32, 64), BF16)
    act_tail[:, 35 * 8 :, :] = jnp.zeros((5, 56, 128), F32)

    def activate(t):
        def one(r, x):
            n = x * rms_scale(x) * gain1[...]
            act_rows[r] = n * sigmoid(n)

        def run(b):
            for r in range(2):
                x = jnp.where(b == 0, before[t, r].astype(F32), after[t, r].astype(F32))
                one(r, x)
            for r in range(16):
                i = 16 * b + r
                one(r + 2, jnp.concatenate([feat[t, i].astype(F32), feat_side[t, i].astype(F32)], axis=0))
            for r in range(18):
                put_row(act[t], act_tail, r + 34 * b if r < 2 else r + 16 * b, act_rows[r])

        return run

    def first_conv(t):
        frames = range(max(0, t - 2), t + 1)

        def run(b):
            w = jnp.concatenate([weight_rows(w1, s - t + 2) for s in frames], axis=0)
            lhs = operand(act, act_strip, frames, 17 * b, 17, 2 * b)
            value = conv_dot(lhs, w, 0)
            split(value, b, pre.at[t], pre_strip.at[t], bias[...].reshape(1, 1, 192))

        return run

    done = lambda t: lambda: build_strip(act_strip[t], act_tail)
    run_steps(
        [
            ([activate(0)], [done(0)]),
            ([first_conv(0), activate(1)], [done(1)]),
            ([first_conv(1), activate(2)], [done(2)]),
            ([first_conv(2), activate(3)], [done(3)]),
            ([first_conv(3)], []),
        ]
    )


def backward(*refs):
    flags, feat, pre, pre_strip, cot, cot_side, before, after, w1, w2, wup, gain1, gain2, out = refs[:14]
    act, grad, grad_strip, block = (refs[14 + 4 * n : 18 + 4 * n] for n in range(4))
    acc_up, acc, acc_strip, pooled = (refs[30 + 2 * n : 32 + 2 * n] for n in range(4))
    acc_last = (refs[38], acc_up[1], acc_up[0], refs[38])
    grad_tail, grad_rows, edges, line, mask, strip_mask, w2t, w1t, wu = refs[39:]

    for n in range(4):
        act[n][35, :, 576:640] = jnp.zeros((32, 64), BF16)
        grad[n][35, :, 576:640] = jnp.zeros((32, 64), BF16)
    grad_tail[:, 35 * 8 :, :] = jnp.zeros((5, 56, 128), F32)
    line[...] = jnp.zeros_like(line)
    s = lax.broadcasted_iota(jnp.int32, mask.shape, 0)
    good = (s < 32) | ((s < 34) & (flags[3] > 0)) | ((s >= 38) & (flags[2] > 0))
    mask[...] = jnp.where(good, 1.0, 0.0)
    r, s = (lax.broadcasted_iota(jnp.int32, strip_mask.shape, n) for n in range(2))
    o = DEEP * lax.rem(s, 8) + r
    good = jnp.where(s < 8, flags[2], flags[3]) > 0
    good &= ((o > 0) | (flags[0] > 0)) & ((o < 33) | (flags[1] > 0))
    strip_mask[...] = jnp.where(good, 1.0, 0.0)
    pack_adjoint(w2t, w2)
    pack_adjoint(w1t, w1)
    for p in range(3):
        for q in range(3):
            tap = 128 * (3 * p + q)
            wu[:, tap : tap + 96] = wup[2 - p, 2 - q]
            wu[:, tap + 96 : tap + 128] = jnp.zeros((192, 32), BF16)

    def edge(value, b, r, first, last):
        if r in first:
            return value * jnp.where((b == 0) & (flags[0] == 0), 0.0, 1.0)
        if r in last:
            return value * jnp.where((b == 1) & (flags[1] == 0), 0.0, 1.0)
        return value

    def pool(t):
        dst = pooled[t % 2]

        def own(y):
            return jnp.concatenate([cot[t, y], cot_side[t, y]], axis=0).astype(F32)

        def one(e, rows, slot):
            for m in range(2):
                line[slot, m, :, 0:96] = rows[m] + rows[m + 1]
                even = line[slot, m, pl.ds(0, 40, stride=2), :]
                odd = line[slot, m, pl.ds(1, 40, stride=2), :]
                dst[m, e, :COLS, 0:128] = (pltpu.roll(odd, 1, 0) + even).astype(BF16)
                dst[m, e, :COLS, 128:256] = (even + odd).astype(BF16)
                dst[m, e, :COLS, 256:384] = (odd + pltpu.roll(even, 39, 0)).astype(BF16)

        def run(b):
            top = [before[t, r].astype(F32) for r in range(5)] + [own(0), own(1)]
            low = [own(63)] + [after[t, r].astype(F32) for r in range(5)]
            low.append(low[-1])
            ends = [jnp.where(b == 0, x, y) for x, y in zip(top, low)]
            for r in range(3):
                one(34 * b + r, ends[2 * r : 2 * r + 3], r)
            for r in range(16):
                e = jnp.minimum(3 + 16 * b + r, 33)
                one(e, [own(2 * e - 5 + m) for m in range(3)], 3 + r % 13)

        return run

    def keep_block(t):
        def run(b):
            for r in range(18):
                e = 18 * b + r
                value = edge(acc_up[t % 2][e] * mask[...], b, r, (0, 1), (16, 17))
                put_row(grad[t], grad_tail, e, value)
                block[t][e] = value[:32]

        return run

    def norm_back(v, gain, top):
        scale = rms_scale(v)
        n = v * scale * gain
        s = sigmoid(n)
        u = gain * (top * (s * (1.0 + n * (1.0 - s))))
        mean = jnp.sum(v * u, axis=-1, keepdims=True) * (1.0 / 192)
        return scale * u - v * (scale * scale * scale * mean)

    def strip_grad(t):
        g = norm_back(pre_strip[t], gain2[...].reshape(1, 1, 192), acc_strip[t % 2][...])
        g = g * strip_mask[...]
        for r in range(DEEP):
            edges[16 * r : 16 * r + 16, :] = g[r]

    def pre_grad(t):
        spot = lax.broadcasted_iota(jnp.int32, (8, 192), 0)

        def run(b):
            for r in range(17):
                o = 17 * b + r
                g = norm_back(pre[t, o], gain2[...], acc[t % 2][o])
                at = 16 * lax.rem(o, DEEP) + lax.div(o, DEEP)
                left, right = edges[pl.ds(at, 1), :], edges[pl.ds(at + 8, 1), :]
                grad_rows[r, :32] = edge(g, b, r, (0,), (16,))
                grad_rows[r, 32:] = jnp.where(spot == 0, right, jnp.where(spot == 7, left, 0.0))
            for r in range(17):
                put_row(act[t], None, 17 * b + r, grad_rows[r])

        return run

    def finish(t):
        def run(b):
            for r in range(16):
                i = 16 * b + r
                g = norm_back(feat[t, i].astype(F32), gain1[...], acc_last[t][i, :32])
                out[t, i] = (block[t][i + 2] + g).astype(BF16)

        return run

    def transposed(lhs, w, frames):
        return conv_dot(lhs, jnp.concatenate([w[s - frames[0]] for s in frames], axis=1), 1)

    def second(t):
        frames = range(t, min(4, t + 3))

        def run(b):
            value = transposed(operand(grad, grad_strip, frames, 17 * b, 17, 2 * b), w2t, frames)
            split(value, b, acc[t % 2], acc_strip[t % 2], 0.0)

        return run

    def last(t):
        frames = range(t, min(4, t + 3))

        def run(b):
            value = transposed(operand(act, None, frames, 16 * b, 16, 0), w1t, frames)
            acc_last[t][pl.ds(16 * b, 16), :32] = value.reshape(16, 32, 192)

        return run

    def up_conv(t):
        src = pooled[t % 2]

        def run(b):
            parts = [src[0, pl.ds(18 * b, 18)], src[1, pl.ds(18 * b, 18)], src[0, pl.ds(18 * b + 1, 18)]]
            lhs = jnp.concatenate([x.reshape(18 * WIDE, 384) for x in parts], axis=1)
            value = conv_dot(lhs, wu[...], 1)
            acc_up[t % 2][pl.ds(18 * b, 18)] = value.reshape(18, WIDE, 192)[:, :COLS]

        return run

    grad_done = lambda t: lambda: build_strip(grad_strip[t], grad_tail)
    second_done = lambda t: lambda: strip_grad(t)
    run_steps(
        [
            ([pool(3)], []),
            ([up_conv(3), pool(2)], []),
            ([up_conv(2), keep_block(3), pool(1)], [grad_done(3)]),
            ([second(3), up_conv(1), keep_block(2), pool(0)], [grad_done(2), second_done(3)]),
            ([second(2), up_conv(0), keep_block(1), pre_grad(3)], [grad_done(1), second_done(2)]),
            ([last(3), second(1), keep_block(0), pre_grad(2)], [grad_done(0), second_done(1)]),
            ([second(0), last(2), pre_grad(1), finish(3)], [second_done(0)]),
            ([last(1), pre_grad(0), finish(2)], []),
            ([last(0), finish(1)], []),
            ([finish(0)], []),
        ]
    )


def per_device(
    features, conv_first, bias_first, gain_first, conv_second, gain_second, up_weight, cotangent
):
    left, right = shift_pair(features[:, :, 30:], features[:, :, :2], "wa")
    gap = jnp.zeros(left.shape[:2] + (4, 192), BF16)
    feat_side = jnp.concatenate([right, gap, left], axis=2)
    cot_left, cot_right = shift_pair(cotangent[:, :, 56:], cotangent[:, :, :8], "wa")
    cot_side = jnp.concatenate([cot_right, cot_left], axis=2)

    def rows(field, side, lo, count):
        part = slice(lo, lo + count)
        return jnp.concatenate([field[:, part], side[:, part]], axis=2)

    before, after = shift_pair(rows(features, feat_side, 30, 2), rows(features, feat_side, 0, 2), "ha")
    cot_up, cot_down = rows(cotangent, cot_side, 59, 5), rows(cotangent, cot_side, 0, 5)
    before, after, cot_up, cot_down = lax.optimization_barrier((before, after, cot_up, cot_down))
    cot_before, cot_after = shift_pair(cot_up, cot_down, "ha")

    bias, gain1, gain2 = (x.reshape(1, 192) for x in (bias_first, gain_first, gain_second))
    ha, wa = lax.axis_index("ha"), lax.axis_index("wa")
    flags = jnp.stack(
        [ha > 0, ha < lax.axis_size("ha") - 1, wa > 0, wa < lax.axis_size("wa") - 1]
    ).astype(jnp.int32)
    vmem = pl.BlockSpec(memory_space=pltpu.VMEM)
    pre, pre_strip = pl.pallas_call(
        forward,
        out_shape=[
            jax.ShapeDtypeStruct((4, 34, 32, 192), F32),
            jax.ShapeDtypeStruct((4, DEEP, 16, 192), F32),
        ],
        in_specs=[vmem] * 7,
        out_specs=[vmem] * 2,
        scratch_shapes=[pltpu.VMEM((36, 32, 640), BF16)] * 4
        + [pltpu.VMEM((DEEP + 2, 16, 640), BF16)] * 4
        + [pltpu.VMEM((5, 8 * (7 + 7 * DEEP), 128), F32), pltpu.VMEM((18, COLS, 192), F32)],
        compiler_params=pltpu.CompilerParams(vmem_limit_bytes=28 * 1024 * 1024),
        cost_estimate=pl.CostEstimate(flops=20_000_000_000, transcendentals=1_000_000, bytes_accessed=12_000_000),
        name="forward_block",
    )(features, feat_side, before, after, conv_first, bias, gain1)
    return pl.pallas_call(
        backward,
        out_shape=jax.ShapeDtypeStruct(features.shape, BF16),
        in_specs=[pl.BlockSpec(memory_space=pltpu.SMEM)] + [vmem] * 12,
        out_specs=vmem,
        scratch_shapes=[pltpu.VMEM((36, 32, 640), BF16)] * 8
        + [pltpu.VMEM((DEEP + 2, 16, 640), BF16)] * 4
        + [pltpu.VMEM((36, 32, 192), F32)] * 4
        + [pltpu.VMEM((36, COLS, 192), F32)] * 2
        + [pltpu.VMEM((34, 32, 192), F32)] * 2
        + [pltpu.VMEM((DEEP, 16, 192), F32)] * 2
        + [pltpu.VMEM((2, 37, WIDE, 384), BF16)] * 2
        + [pltpu.VMEM((32, 32, 192), F32)]
        + [
            pltpu.VMEM((5, 8 * (7 + 7 * DEEP), 128), F32),
            pltpu.VMEM((17, COLS, 192), F32),
            pltpu.VMEM((16 * DEEP, 192), F32),
            pltpu.VMEM((16, 2, 80, 128), F32),
            pltpu.VMEM((COLS, 192), F32),
            pltpu.VMEM((DEEP, 16, 192), F32),
            pltpu.VMEM((3, 192, 1792), BF16),
            pltpu.VMEM((3, 192, 1792), BF16),
            pltpu.VMEM((192, 1152), BF16),
        ],
        compiler_params=pltpu.CompilerParams(vmem_limit_bytes=58 * 1024 * 1024),
        name="backward_block",
    )(
        flags, features, pre, pre_strip, cotangent, cot_side, cot_before, cot_after, conv_first,
        conv_second, up_weight, gain1, gain2,
    )


def solution(mesh):
    placed = (P(None, "ha", "wa", None), P(), P(), P(), P(), P(), P(), P(None, "ha", "wa", None))
    return jax.shard_map(
        per_device, mesh=mesh, in_specs=placed, out_specs=P(None, "ha", "wa", None), check_vma=False
    )
```

```python
import jax
import jax.numpy as jnp
from jax import lax
from jax.experimental import pallas as pl
from jax.experimental.pallas import tpu as pltpu
from jax.sharding import PartitionSpec as P

COLS = 40
WIDE = 48
DEEP = 5
LANES = (640, 512, 640)
F32 = jnp.float32
BF16 = jnp.bfloat16


def shift_pair(value_up, value_down, axis):
    count = lax.axis_size(axis)
    up = [(i, (i + 1) % count) for i in range(count - 1)]
    down = [(j, i) for i, j in up]
    return lax.ppermute(value_up, axis, up), lax.ppermute(value_down, axis, down)


def rms_scale(value):
    return lax.rsqrt(jnp.sum(value * value, axis=-1, keepdims=True) * (1.0 / 192) + 1e-06)


def sigmoid(value):
    return 0.5 * jnp.tanh(0.5 * value) + 0.5


def put_row(ref, tail, e, value):
    low, high = value[:, :128], value[:, 128:]
    high = jnp.concatenate([high, high], axis=1)
    lane = lax.broadcasted_iota(jnp.int32, high.shape, 1)
    left = jnp.where(lane < 64, pltpu.roll(high, 1, 0), high)
    after = pltpu.roll(high, COLS - 1, 0)
    before = jnp.maximum(e - 1, 0)
    for n, x in enumerate([pltpu.roll(low, 1, 0), low, pltpu.roll(low, COLS - 1, 0), left]):
        ref[e, :, 128 * n : 128 * n + 128] = x[:32].astype(BF16)
        if tail is not None:
            tail[n, pl.ds(8 * e, 8), :] = x[32:]
    own = after[:32].astype(BF16)
    ref[e, :, 512:576] = own[:, :64]
    ref[before, :, 576:640] = own[:, 64:]
    if tail is not None:
        tail[4, pl.ds(8 * e, 8), 0:64] = after[32:, :64]
        tail[4, pl.ds(8 * before, 8), 64:128] = after[32:, 64:]


def build_strip(dst, tail):
    for r in range(DEEP + 2):
        for n in range(5):
            sides = [tail[n, pl.ds(8 * r + first, 8, stride=8 * DEEP), :] for first in (7, 0)]
            dst[r, :, 128 * n : 128 * n + 128] = jnp.concatenate(sides, axis=0).astype(BF16)


def weight_rows(w_ref, k):
    rows = []
    for p in range(3):
        w = [w_ref[k, p, q] for q in range(3)]
        rows += [w[0][:128], w[1][:128], w[2][:128], w[0][128:], w[1][128:]]
        if p == 0:
            rows += [w[2][128:], w_ref[k, 1, 2, 128:, :]]
        if p == 2:
            rows += [w[2][128:], jnp.zeros((64, 192), BF16)]
    return jnp.concatenate(rows, axis=0)


def pack_adjoint(dst, w_ref):
    for k in range(3):
        base = 0
        for p in range(3):
            w = [w_ref[2 - k, 2 - p, 2 - q] for q in range(3)]
            for q in range(3):
                dst[k, :, base + 128 * q : base + 128 * q + 128] = w[q][:, :128]
            dst[k, :, base + 384 : base + 512] = jnp.concatenate([w[0][:, 128:], w[1][:, 128:]], axis=1)
            if p != 1:
                other = w_ref[2 - k, 1, 0][:, 128:] if p == 0 else jnp.zeros((192, 64), BF16)
                dst[k, :, base + 512 : base + 640] = jnp.concatenate([w[2][:, 128:], other], axis=1)
            base += LANES[p]


def operand(refs, strips, frames, row, rows, strip_row):
    parts = []
    for s in frames:
        for p in range(3):
            lanes = LANES[p]
            piece = refs[s][pl.ds(row + p, rows), :, 0:lanes].reshape(rows * 32, lanes)
            if strips is not None:
                side = strips[s][pl.ds(strip_row + p, 3), :, 0:lanes].reshape(48, lanes)
                piece = jnp.concatenate([piece, side], axis=0)
            parts.append(piece)
    return jnp.concatenate(parts, axis=1)


def conv_dot(lhs, w, axis):
    return lax.dot_general(lhs, w, (((1,), (axis,)), ((), ())), preferred_element_type=F32)


def split(value, b, main, strip, add):
    main[pl.ds(17 * b, 17)] = value[: 17 * 32].reshape(17, 32, 192) + add
    strip[pl.ds(2 * b, 3)] = value[17 * 32 :].reshape(3, 16, 192) + add


def run_steps(steps):
    for jobs, then in steps:

        def step(b, carry):
            for job in jobs:
                job(b)
            return carry

        lax.fori_loop(0, 2, step, 0)
        for job in then:
            job()


def forward(*refs):
    feat_in, feat_side, before, after, w1_in, bias, gain1, pre_out, pre_strip = refs[:9]
    act, act_strip = refs[9:13], refs[13:17]
    act_tail, act_rows, pre, feat, w1, sem = refs[17:]
    load_feat = [pltpu.make_async_copy(feat_in.at[t], feat.at[t], sem.at[4 + t]) for t in range(4)]
    load_w1 = pltpu.make_async_copy(w1_in, w1, sem.at[8])
    for copy in (load_feat[0], load_w1, *load_feat[1:]):
        copy.start()
    stores = [pltpu.make_async_copy(pre.at[t], pre_out.at[t], sem.at[t]) for t in range(4)]
    for n in range(4):
        act[n][35, :, 576:640] = jnp.zeros((32, 64), BF16)
    act_tail[:, 35 * 8 :, :] = jnp.zeros((5, 56, 128), F32)

    def activate(t):
        def one(r, x):
            n = x * rms_scale(x) * gain1[...]
            act_rows[r] = n * sigmoid(n)

        def run(b):
            for r in range(2):
                x = jnp.where(b == 0, before[t, r].astype(F32), after[t, r].astype(F32))
                one(r, x)
            for r in range(16):
                i = 16 * b + r
                one(r + 2, jnp.concatenate([feat[t, i].astype(F32), feat_side[t, i].astype(F32)], axis=0))
            for r in range(18):
                put_row(act[t], act_tail, r + 34 * b if r < 2 else r + 16 * b, act_rows[r])

        return run

    def first_conv(t):
        frames = range(max(0, t - 2), t + 1)

        def run(b):
            w = jnp.concatenate([weight_rows(w1, s - t + 2) for s in frames], axis=0)
            lhs = operand(act, act_strip, frames, 17 * b, 17, 2 * b)
            value = conv_dot(lhs, w, 0)
            split(value, b, pre.at[t], pre_strip.at[t], bias[...].reshape(1, 1, 192))

        return run

    done = lambda t: lambda: build_strip(act_strip[t], act_tail)
    load_feat[0].wait()
    run_steps(
        [
            ([activate(0)], [done(0), load_w1.wait, load_feat[1].wait]),
            ([first_conv(0), activate(1)], [done(1), stores[0].start, load_feat[2].wait]),
            ([first_conv(1), activate(2)], [done(2), stores[1].start, load_feat[3].wait]),
            ([first_conv(2), activate(3)], [done(3), stores[2].start]),
            ([first_conv(3)], [stores[3].start]),
        ]
    )
    for copy in stores:
        copy.wait()


def backward(*refs):
    flags, feat_in, pre_in, pre_strip, cot_in, cot_side, before, after, w1_in, w2_in = refs[:10]
    wup, gain1, gain2, result = refs[10:14]
    act, grad, grad_strip, block = (refs[14 + 4 * n : 18 + 4 * n] for n in range(4))
    acc_up, acc, acc_strip, pooled = (refs[30 + 2 * n : 32 + 2 * n] for n in range(4))
    acc_last = (refs[38], acc_up[1], acc_up[0], refs[38])
    grad_tail, grad_rows, edges, line, mask, strip_mask, w2t, w1t, wu = refs[39:48]
    feat, pre, cot, w1, w2, out, sem = refs[48:]

    def copies(src, dst, first):
        return [pltpu.make_async_copy(src.at[t], dst.at[t], sem.at[first + t]) for t in range(4)]

    load_cot, load_pre, store = copies(cot_in, cot, 0), copies(pre_in, pre, 4), copies(out, result, 8)
    load_w2 = pltpu.make_async_copy(w2_in, w2, sem.at[12])
    load_w1 = pltpu.make_async_copy(w1_in, w1, sem.at[13])
    load_feat = pltpu.make_async_copy(feat_in, feat, sem.at[14])
    for copy in (load_cot[3], load_w2, load_cot[2], load_cot[1], load_cot[0], load_pre[3], load_w1):
        copy.start()
    for copy in (load_pre[2], load_pre[1], load_feat, load_pre[0]):
        copy.start()

    for n in range(4):
        act[n][35, :, 576:640] = jnp.zeros((32, 64), BF16)
        grad[n][35, :, 576:640] = jnp.zeros((32, 64), BF16)
    grad_tail[:, 35 * 8 :, :] = jnp.zeros((5, 56, 128), F32)
    line[...] = jnp.zeros_like(line)
    s = lax.broadcasted_iota(jnp.int32, mask.shape, 0)
    good = (s < 32) | ((s < 34) & (flags[3] > 0)) | ((s >= 38) & (flags[2] > 0))
    mask[...] = jnp.where(good, 1.0, 0.0)
    r, s = (lax.broadcasted_iota(jnp.int32, strip_mask.shape, n) for n in range(2))
    o = DEEP * lax.rem(s, 8) + r
    good = jnp.where(s < 8, flags[2], flags[3]) > 0
    good &= ((o > 0) | (flags[0] > 0)) & ((o < 33) | (flags[1] > 0))
    strip_mask[...] = jnp.where(good, 1.0, 0.0)
    for p in range(3):
        for q in range(3):
            tap = 128 * (3 * p + q)
            wu[:, tap : tap + 96] = wup[2 - p, 2 - q]
            wu[:, tap + 96 : tap + 128] = jnp.zeros((192, 32), BF16)

    def edge(value, b, r, first, last):
        if r in first:
            return value * jnp.where((b == 0) & (flags[0] == 0), 0.0, 1.0)
        if r in last:
            return value * jnp.where((b == 1) & (flags[1] == 0), 0.0, 1.0)
        return value

    def pool(t):
        dst = pooled[t % 2]

        def own(y):
            return jnp.concatenate([cot[t, y], cot_side[t, y]], axis=0).astype(F32)

        def one(e, rows, slot):
            for m in range(2):
                line[slot, m, :, 0:96] = rows[m] + rows[m + 1]
                even = line[slot, m, pl.ds(0, 40, stride=2), :]
                odd = line[slot, m, pl.ds(1, 40, stride=2), :]
                dst[m, e, :COLS, 0:128] = (pltpu.roll(odd, 1, 0) + even).astype(BF16)
                dst[m, e, :COLS, 128:256] = (even + odd).astype(BF16)
                dst[m, e, :COLS, 256:384] = (odd + pltpu.roll(even, 39, 0)).astype(BF16)

        def run(b):
            top = [before[t, r].astype(F32) for r in range(5)] + [own(0), own(1)]
            low = [own(63)] + [after[t, r].astype(F32) for r in range(5)]
            low.append(low[-1])
            ends = [jnp.where(b == 0, x, y) for x, y in zip(top, low)]
            for r in range(3):
                one(34 * b + r, ends[2 * r : 2 * r + 3], r)
            for r in range(16):
                e = jnp.minimum(3 + 16 * b + r, 33)
                one(e, [own(2 * e - 5 + m) for m in range(3)], 3 + r % 13)

        return run

    def keep_block(t):
        def run(b):
            for r in range(18):
                e = 18 * b + r
                value = edge(acc_up[t % 2][e] * mask[...], b, r, (0, 1), (16, 17))
                put_row(grad[t], grad_tail, e, value)
                block[t][e] = value[:32]

        return run

    def norm_back(v, gain, top):
        scale = rms_scale(v)
        n = v * scale * gain
        s = sigmoid(n)
        u = gain * (top * (s * (1.0 + n * (1.0 - s))))
        mean = jnp.sum(v * u, axis=-1, keepdims=True) * (1.0 / 192)
        return scale * u - v * (scale * scale * scale * mean)

    def strip_grad(t):
        g = norm_back(pre_strip[t], gain2[...].reshape(1, 1, 192), acc_strip[t % 2][...])
        g = g * strip_mask[...]
        for r in range(DEEP):
            edges[16 * r : 16 * r + 16, :] = g[r]

    def pre_grad(t):
        spot = lax.broadcasted_iota(jnp.int32, (8, 192), 0)

        def run(b):
            for r in range(17):
                o = 17 * b + r
                g = norm_back(pre[t, o], gain2[...], acc[t % 2][o])
                at = 16 * lax.rem(o, DEEP) + lax.div(o, DEEP)
                left, right = edges[pl.ds(at, 1), :], edges[pl.ds(at + 8, 1), :]
                grad_rows[r, :32] = edge(g, b, r, (0,), (16,))
                grad_rows[r, 32:] = jnp.where(spot == 0, right, jnp.where(spot == 7, left, 0.0))
            for r in range(17):
                put_row(act[t], None, 17 * b + r, grad_rows[r])

        return run

    def finish(t):
        def run(b):
            for r in range(16):
                i = 16 * b + r
                g = norm_back(feat[t, i].astype(F32), gain1[...], acc_last[t][i, :32])
                out[t, i] = (block[t][i + 2] + g).astype(BF16)

        return run

    def transposed(lhs, w, frames):
        return conv_dot(lhs, jnp.concatenate([w[s - frames[0]] for s in frames], axis=1), 1)

    def second(t):
        frames = range(t, min(4, t + 3))

        def run(b):
            value = transposed(operand(grad, grad_strip, frames, 17 * b, 17, 2 * b), w2t, frames)
            split(value, b, acc[t % 2], acc_strip[t % 2], 0.0)

        return run

    def last(t):
        frames = range(t, min(4, t + 3))

        def run(b):
            value = transposed(operand(act, None, frames, 16 * b, 16, 0), w1t, frames)
            acc_last[t][pl.ds(16 * b, 16), :32] = value.reshape(16, 32, 192)

        return run

    def up_conv(t):
        src = pooled[t % 2]

        def run(b):
            parts = [src[0, pl.ds(18 * b, 18)], src[1, pl.ds(18 * b, 18)], src[0, pl.ds(18 * b + 1, 18)]]
            lhs = jnp.concatenate([x.reshape(18 * WIDE, 384) for x in parts], axis=1)
            value = conv_dot(lhs, wu[...], 1)
            acc_up[t % 2][pl.ds(18 * b, 18)] = value.reshape(18, WIDE, 192)[:, :COLS]

        return run

    grad_done = lambda t: lambda: build_strip(grad_strip[t], grad_tail)
    second_done = lambda t: lambda: strip_grad(t)
    pack2, pack1 = lambda: pack_adjoint(w2t, w2), lambda: pack_adjoint(w1t, w1)
    load_cot[3].wait()
    run_steps(
        [
            ([pool(3)], [load_cot[2].wait]),
            ([up_conv(3), pool(2)], [load_cot[1].wait]),
            ([up_conv(2), keep_block(3), pool(1)], [grad_done(3), load_w2.wait, pack2, load_cot[0].wait]),
            (
                [second(3), up_conv(1), keep_block(2), pool(0)],
                [grad_done(2), load_pre[3].wait, second_done(3)],
            ),
            (
                [second(2), up_conv(0), keep_block(1), pre_grad(3)],
                [grad_done(1), second_done(2), load_w1.wait, pack1, load_pre[2].wait],
            ),
            (
                [last(3), second(1), keep_block(0), pre_grad(2)],
                [grad_done(0), second_done(1), load_pre[1].wait, load_feat.wait],
            ),
            (
                [second(0), last(2), pre_grad(1), finish(3)],
                [second_done(0), load_pre[0].wait, store[3].start],
            ),
            ([last(1), pre_grad(0), finish(2)], [store[2].start]),
            ([last(0), finish(1)], [store[1].start]),
            ([finish(0)], [store[0].start]),
        ]
    )
    for copy in store:
        copy.wait()


def halves(field, axis):
    half = field.shape[-1] // 2
    return jnp.concatenate([field[..., :half], field[..., half:]], axis=axis)


def per_device(
    features, conv_first, bias_first, gain_first, conv_second, gain_second, up_weight, cotangent
):
    def cols(lo_f, lo_c):
        parts = [cotangent[:, :, lo_c : lo_c + 5], halves(features[:, :, lo_f : lo_f + 2], 1)]
        return jnp.pad(jnp.concatenate(parts, axis=2), ((0, 0), (0, 0), (0, 1), (0, 0)))

    left, right = shift_pair(cols(30, 59), cols(0, 0), "wa")

    def ring(first, last, width):
        gap = jnp.zeros(first.shape[:2] + (width - 2 * first.shape[2], first.shape[3]), BF16)
        return jnp.concatenate([first, gap, last], axis=2)

    cot_side = ring(right[:, :, :5], left[:, :, :5], 16)
    whole = lambda side: jnp.concatenate([side[:, :32, 5:7], side[:, 32:, 5:7]], axis=3)
    feat_side = ring(whole(right), whole(left), 8)

    def rows(field, side, lo, count):
        part = slice(lo, lo + count)
        return jnp.concatenate([field[:, part], side[:, part]], axis=2)

    up, down = rows(features, feat_side, 30, 2), rows(features, feat_side, 0, 2)
    cot_up, cot_down = rows(cotangent, cot_side, 59, 5), rows(cotangent, cot_side, 0, 5)
    up, down, cot_up, cot_down = lax.optimization_barrier((up, down, cot_up, cot_down))
    before, after = shift_pair(up, down, "ha")
    cot_before, cot_after = shift_pair(cot_up, cot_down, "ha")

    bias, gain1, gain2 = (x.reshape(1, 192) for x in (bias_first, gain_first, gain_second))
    ha, wa = lax.axis_index("ha"), lax.axis_index("wa")
    flags = jnp.stack(
        [ha > 0, ha < lax.axis_size("ha") - 1, wa > 0, wa < lax.axis_size("wa") - 1]
    ).astype(jnp.int32)
    vmem, own = pl.BlockSpec(memory_space=pltpu.VMEM), pl.BlockSpec(memory_space=pltpu.HBM)
    pre, pre_strip = pl.pallas_call(
        forward,
        out_shape=[
            jax.ShapeDtypeStruct((4, 34, 32, 192), F32),
            jax.ShapeDtypeStruct((4, DEEP, 16, 192), F32),
        ],
        in_specs=[own] + [vmem] * 3 + [own] + [vmem] * 2,
        out_specs=[own, vmem],
        scratch_shapes=[pltpu.VMEM((36, 32, 640), BF16)] * 4
        + [pltpu.VMEM((DEEP + 2, 16, 640), BF16)] * 4
        + [pltpu.VMEM((5, 8 * (7 + 7 * DEEP), 128), F32), pltpu.VMEM((18, COLS, 192), F32)]
        + [
            pltpu.VMEM((4, 34, 32, 192), F32),
            pltpu.VMEM((4, 32, 32, 192), BF16),
            pltpu.VMEM((3, 3, 3, 192, 192), BF16),
            pltpu.SemaphoreType.DMA((9,)),
        ],
        compiler_params=pltpu.CompilerParams(vmem_limit_bytes=60 * 1024 * 1024),
        cost_estimate=pl.CostEstimate(flops=20_000_000_000, transcendentals=1_000_000, bytes_accessed=12_000_000),
        name="forward_block",
    )(features, feat_side, before, after, conv_first, bias, gain1)
    return pl.pallas_call(
        backward,
        out_shape=jax.ShapeDtypeStruct(features.shape, BF16),
        in_specs=[pl.BlockSpec(memory_space=pltpu.SMEM), own, own, vmem, own] + [vmem] * 3
        + [own, own] + [vmem] * 3,
        out_specs=own,
        scratch_shapes=[pltpu.VMEM((36, 32, 640), BF16)] * 8
        + [pltpu.VMEM((DEEP + 2, 16, 640), BF16)] * 4
        + [pltpu.VMEM((36, 32, 192), F32)] * 4
        + [pltpu.VMEM((36, COLS, 192), F32)] * 2
        + [pltpu.VMEM((34, 32, 192), F32)] * 2
        + [pltpu.VMEM((DEEP, 16, 192), F32)] * 2
        + [pltpu.VMEM((2, 37, WIDE, 384), BF16)] * 2
        + [pltpu.VMEM((32, 32, 192), F32)]
        + [
            pltpu.VMEM((5, 8 * (7 + 7 * DEEP), 128), F32),
            pltpu.VMEM((17, COLS, 192), F32),
            pltpu.VMEM((16 * DEEP, 192), F32),
            pltpu.VMEM((16, 2, 80, 128), F32),
            pltpu.VMEM((COLS, 192), F32),
            pltpu.VMEM((DEEP, 16, 192), F32),
            pltpu.VMEM((3, 192, 1792), BF16),
            pltpu.VMEM((3, 192, 1792), BF16),
            pltpu.VMEM((192, 1152), BF16),
            pltpu.VMEM((4, 32, 32, 192), BF16),
            pltpu.VMEM((4, 34, 32, 192), F32),
            pltpu.VMEM((4, 64, 64, 96), BF16),
            pltpu.VMEM((3, 3, 3, 192, 192), BF16),
            pltpu.VMEM((3, 3, 3, 192, 192), BF16),
            pltpu.VMEM((4, 32, 32, 192), BF16),
            pltpu.SemaphoreType.DMA((15,)),
        ],
        compiler_params=pltpu.CompilerParams(vmem_limit_bytes=58 * 1024 * 1024),
        name="backward_block",
    )(
        flags, features, pre, pre_strip, cotangent, cot_side, cot_before, cot_after, conv_first,
        conv_second, up_weight, gain1, gain2,
    )


def solution(mesh):
    placed = (P(None, "ha", "wa", None), P(), P(), P(), P(), P(), P(), P(None, "ha", "wa", None))
    return jax.shard_map(
        per_device, mesh=mesh, in_specs=placed, out_specs=P(None, "ha", "wa", None), check_vma=False
    )
```

```python
import jax
import jax.numpy as jnp
from jax import lax
from jax.experimental import pallas as pl
from jax.experimental.pallas import tpu as pltpu
from jax.sharding import PartitionSpec as P

COLS = 40
WIDE = 48
DEEP = 5
LANES = (640, 512, 640)
F32 = jnp.float32
BF16 = jnp.bfloat16


def shift_pair(value_up, value_down, axis):
    count = lax.axis_size(axis)
    up = [(i, (i + 1) % count) for i in range(count - 1)]
    down = [(j, i) for i, j in up]
    return lax.ppermute(value_up, axis, up), lax.ppermute(value_down, axis, down)


def rms_scale(value):
    return lax.rsqrt(jnp.sum(value * value, axis=-1, keepdims=True) * (1.0 / 192) + 1e-06)


def sigmoid(value):
    return 0.5 * jnp.tanh(0.5 * value) + 0.5


def put_row(ref, tail, e, value):
    low, high = value[:, :128], value[:, 128:]
    high = jnp.concatenate([high, high], axis=1)
    lane = lax.broadcasted_iota(jnp.int32, high.shape, 1)
    left = jnp.where(lane < 64, pltpu.roll(high, 1, 0), high)
    after = pltpu.roll(high, COLS - 1, 0)
    before = jnp.maximum(e - 1, 0)
    for n, x in enumerate([pltpu.roll(low, 1, 0), low, pltpu.roll(low, COLS - 1, 0), left]):
        ref[e, :, 128 * n : 128 * n + 128] = x[:32].astype(BF16)
        if tail is not None:
            tail[n, pl.ds(8 * e, 8), :] = x[32:]
    own = after[:32].astype(BF16)
    ref[e, :, 512:576] = own[:, :64]
    ref[before, :, 576:640] = own[:, 64:]
    if tail is not None:
        tail[4, pl.ds(8 * e, 8), 0:64] = after[32:, :64]
        tail[4, pl.ds(8 * before, 8), 64:128] = after[32:, 64:]


def build_strip(dst, tail):
    for r in range(DEEP + 2):
        for n in range(5):
            sides = [tail[n, pl.ds(8 * r + first, 8, stride=8 * DEEP), :] for first in (7, 0)]
            dst[r, :, 128 * n : 128 * n + 128] = jnp.concatenate(sides, axis=0).astype(BF16)


def weight_rows(w_ref, k):
    rows = []
    for p in range(3):
        w = [w_ref[k, p, q] for q in range(3)]
        rows += [w[0][:128], w[1][:128], w[2][:128], w[0][128:], w[1][128:]]
        if p == 0:
            rows += [w[2][128:], w_ref[k, 1, 2, 128:, :]]
        if p == 2:
            rows += [w[2][128:], jnp.zeros((64, 192), BF16)]
    return jnp.concatenate(rows, axis=0)


def pack_adjoint(dst, w_ref):
    for k in range(3):
        base = 0
        for p in range(3):
            w = [w_ref[2 - k, 2 - p, 2 - q] for q in range(3)]
            for q in range(3):
                dst[k, :, base + 128 * q : base + 128 * q + 128] = w[q][:, :128]
            dst[k, :, base + 384 : base + 512] = jnp.concatenate([w[0][:, 128:], w[1][:, 128:]], axis=1)
            if p != 1:
                other = w_ref[2 - k, 1, 0][:, 128:] if p == 0 else jnp.zeros((192, 64), BF16)
                dst[k, :, base + 512 : base + 640] = jnp.concatenate([w[2][:, 128:], other], axis=1)
            base += LANES[p]


def pack_weights(w1, w2, wup, w1t, w2t, wu):
    pack_adjoint(w2t, w2)
    pack_adjoint(w1t, w1)
    for p in range(3):
        for q in range(3):
            tap = 128 * (3 * p + q)
            wu[:, tap : tap + 96] = wup[2 - p, 2 - q]
            wu[:, tap + 96 : tap + 128] = jnp.zeros((192, 32), BF16)


def operand(refs, strips, frames, row, rows, strip_row):
    parts = []
    for s in frames:
        for p in range(3):
            lanes = LANES[p]
            piece = refs[s][pl.ds(row + p, rows), :, 0:lanes].reshape(rows * 32, lanes)
            if strips is not None:
                side = strips[s][pl.ds(strip_row + p, 3), :, 0:lanes].reshape(48, lanes)
                piece = jnp.concatenate([piece, side], axis=0)
            parts.append(piece)
    return jnp.concatenate(parts, axis=1)


def conv_dot(lhs, w, axis):
    return lax.dot_general(lhs, w, (((1,), (axis,)), ((), ())), preferred_element_type=F32)


def split(value, b, main, strip, add):
    main[pl.ds(17 * b, 17)] = value[: 17 * 32].reshape(17, 32, 192) + add
    strip[pl.ds(2 * b, 3)] = value[17 * 32 :].reshape(3, 16, 192) + add


def run_steps(steps):
    for jobs, then in steps:

        def step(b, carry):
            for job in jobs:
                job(b)
            return carry

        lax.fori_loop(0, 2, step, 0)
        for job in then:
            job()


def forward(*refs):
    feat, feat_side, before, after, w1, bias, gain1, pre_out, pre_strip = refs[:9]
    act, act_strip = refs[9:13], refs[13:17]
    act_tail, act_rows, pre, sem = refs[17:]
    stores = [pltpu.make_async_copy(pre.at[t], pre_out.at[t], sem.at[t]) for t in range(4)]
    for n in range(4):
        act[n][35, :, 576:640] = jnp.zeros((32, 64), BF16)
    act_tail[:, 35 * 8 :, :] = jnp.zeros((5, 56, 128), F32)

    def activate(t):
        def one(r, x):
            n = x * rms_scale(x) * gain1[...]
            act_rows[r] = n * sigmoid(n)

        def run(b):
            for r in range(2):
                x = jnp.where(b == 0, before[t, r].astype(F32), after[t, r].astype(F32))
                one(r, x)
            for r in range(16):
                i = 16 * b + r
                one(r + 2, jnp.concatenate([feat[t, i].astype(F32), feat_side[t, i].astype(F32)], axis=0))
            for r in range(18):
                put_row(act[t], act_tail, r + 34 * b if r < 2 else r + 16 * b, act_rows[r])

        return run

    def first_conv(t):
        frames = range(max(0, t - 2), t + 1)

        def run(b):
            w = jnp.concatenate([weight_rows(w1, s - t + 2) for s in frames], axis=0)
            lhs = operand(act, act_strip, frames, 17 * b, 17, 2 * b)
            value = conv_dot(lhs, w, 0)
            split(value, b, pre.at[t], pre_strip.at[t], bias[...].reshape(1, 1, 192))

        return run

    done = lambda t: lambda: build_strip(act_strip[t], act_tail)
    run_steps(
        [
            ([activate(0)], [done(0)]),
            ([first_conv(0), activate(1)], [done(1), stores[0].start]),
            ([first_conv(1), activate(2)], [done(2), stores[1].start]),
            ([first_conv(2), activate(3)], [done(3), stores[2].start]),
            ([first_conv(3)], [stores[3].start]),
        ]
    )
    for copy in stores:
        copy.wait()


def backward(*refs):
    flags, feat_in, pre_in, pre_strip, cot_in, cot_side, before, after, w1_in, w2_in = refs[:10]
    wu, gain1, gain2, result = refs[10:14]
    act, grad, grad_strip, block = (refs[14 + 4 * n : 18 + 4 * n] for n in range(4))
    acc_up, acc, acc_strip, pooled = (refs[30 + 2 * n : 32 + 2 * n] for n in range(4))
    acc_last = (refs[38], acc_up[1], acc_up[0], refs[38])
    grad_tail, grad_rows, edges, line, mask, strip_mask = refs[39:45]
    feat, pre, cot, w1t, w2t, out, sem = refs[45:]

    def copies(src, dst, first):
        return [pltpu.make_async_copy(src.at[t], dst.at[t], sem.at[first + t]) for t in range(4)]

    load_cot, load_pre, store = copies(cot_in, cot, 0), copies(pre_in, pre, 4), copies(out, result, 8)
    load_w2 = pltpu.make_async_copy(w2_in, w2t, sem.at[12])
    load_w1 = pltpu.make_async_copy(w1_in, w1t, sem.at[13])
    load_feat = pltpu.make_async_copy(feat_in, feat, sem.at[14])
    for copy in (load_cot[3], load_w2, load_cot[2], load_cot[1], load_cot[0], load_pre[3], load_w1):
        copy.start()
    for copy in (load_pre[2], load_pre[1], load_feat, load_pre[0]):
        copy.start()

    for n in range(4):
        act[n][35, :, 576:640] = jnp.zeros((32, 64), BF16)
        grad[n][35, :, 576:640] = jnp.zeros((32, 64), BF16)
    grad_tail[:, 35 * 8 :, :] = jnp.zeros((5, 56, 128), F32)
    line[...] = jnp.zeros_like(line)
    s = lax.broadcasted_iota(jnp.int32, mask.shape, 0)
    good = (s < 32) | ((s < 34) & (flags[3] > 0)) | ((s >= 38) & (flags[2] > 0))
    mask[...] = jnp.where(good, 1.0, 0.0)
    r, s = (lax.broadcasted_iota(jnp.int32, strip_mask.shape, n) for n in range(2))
    o = DEEP * lax.rem(s, 8) + r
    good = jnp.where(s < 8, flags[2], flags[3]) > 0
    good &= ((o > 0) | (flags[0] > 0)) & ((o < 33) | (flags[1] > 0))
    strip_mask[...] = jnp.where(good, 1.0, 0.0)
    def edge(value, b, r, first, last):
        if r in first:
            return value * jnp.where((b == 0) & (flags[0] == 0), 0.0, 1.0)
        if r in last:
            return value * jnp.where((b == 1) & (flags[1] == 0), 0.0, 1.0)
        return value

    def pool(t):
        dst = pooled[t % 2]

        def own(y):
            return jnp.concatenate([cot[t, y], cot_side[t, y]], axis=0).astype(F32)

        def one(e, rows, slot):
            for m in range(2):
                line[slot, m, :, 0:96] = rows[m] + rows[m + 1]
                even = line[slot, m, pl.ds(0, 40, stride=2), :]
                odd = line[slot, m, pl.ds(1, 40, stride=2), :]
                dst[m, e, :COLS, 0:128] = (pltpu.roll(odd, 1, 0) + even).astype(BF16)
                dst[m, e, :COLS, 128:256] = (even + odd).astype(BF16)
                dst[m, e, :COLS, 256:384] = (odd + pltpu.roll(even, 39, 0)).astype(BF16)

        def run(b):
            top = [before[t, r].astype(F32) for r in range(5)] + [own(0), own(1)]
            low = [own(63)] + [after[t, r].astype(F32) for r in range(5)]
            low.append(low[-1])
            ends = [jnp.where(b == 0, x, y) for x, y in zip(top, low)]
            for r in range(3):
                one(34 * b + r, ends[2 * r : 2 * r + 3], r)
            for r in range(16):
                e = jnp.minimum(3 + 16 * b + r, 33)
                one(e, [own(2 * e - 5 + m) for m in range(3)], 3 + r % 13)

        return run

    def keep_block(t):
        def run(b):
            for r in range(18):
                e = 18 * b + r
                value = edge(acc_up[t % 2][e] * mask[...], b, r, (0, 1), (16, 17))
                put_row(grad[t], grad_tail, e, value)
                block[t][e] = value[:32]

        return run

    def norm_back(v, gain, top):
        scale = rms_scale(v)
        n = v * scale * gain
        s = sigmoid(n)
        u = gain * (top * (s * (1.0 + n * (1.0 - s))))
        mean = jnp.sum(v * u, axis=-1, keepdims=True) * (1.0 / 192)
        return scale * u - v * (scale * scale * scale * mean)

    def strip_grad(t):
        g = norm_back(pre_strip[t], gain2[...].reshape(1, 1, 192), acc_strip[t % 2][...])
        g = g * strip_mask[...]
        for r in range(DEEP):
            edges[16 * r : 16 * r + 16, :] = g[r]

    def pre_grad(t):
        spot = lax.broadcasted_iota(jnp.int32, (8, 192), 0)

        def run(b):
            for r in range(17):
                o = 17 * b + r
                g = norm_back(pre[t, o], gain2[...], acc[t % 2][o])
                at = 16 * lax.rem(o, DEEP) + lax.div(o, DEEP)
                left, right = edges[pl.ds(at, 1), :], edges[pl.ds(at + 8, 1), :]
                grad_rows[r, :32] = edge(g, b, r, (0,), (16,))
                grad_rows[r, 32:] = jnp.where(spot == 0, right, jnp.where(spot == 7, left, 0.0))
            for r in range(17):
                put_row(act[t], None, 17 * b + r, grad_rows[r])

        return run

    def finish(t):
        def run(b):
            for r in range(16):
                i = 16 * b + r
                g = norm_back(feat[t, i].astype(F32), gain1[...], acc_last[t][i, :32])
                out[t, i] = (block[t][i + 2] + g).astype(BF16)

        return run

    def transposed(lhs, w, frames):
        return conv_dot(lhs, jnp.concatenate([w[s - frames[0]] for s in frames], axis=1), 1)

    def second(t):
        frames = range(t, min(4, t + 3))

        def run(b):
            value = transposed(operand(grad, grad_strip, frames, 17 * b, 17, 2 * b), w2t, frames)
            split(value, b, acc[t % 2], acc_strip[t % 2], 0.0)

        return run

    def last(t):
        frames = range(t, min(4, t + 3))

        def run(b):
            value = transposed(operand(act, None, frames, 16 * b, 16, 0), w1t, frames)
            acc_last[t][pl.ds(16 * b, 16), :32] = value.reshape(16, 32, 192)

        return run

    def up_conv(t):
        src = pooled[t % 2]

        def run(b):
            parts = [src[0, pl.ds(18 * b, 18)], src[1, pl.ds(18 * b, 18)], src[0, pl.ds(18 * b + 1, 18)]]
            lhs = jnp.concatenate([x.reshape(18 * WIDE, 384) for x in parts], axis=1)
            value = conv_dot(lhs, wu[...], 1)
            acc_up[t % 2][pl.ds(18 * b, 18)] = value.reshape(18, WIDE, 192)[:, :COLS]

        return run

    grad_done = lambda t: lambda: build_strip(grad_strip[t], grad_tail)
    second_done = lambda t: lambda: strip_grad(t)
    load_cot[3].wait()
    run_steps(
        [
            ([pool(3)], [load_cot[2].wait]),
            ([up_conv(3), pool(2)], [load_cot[1].wait]),
            ([up_conv(2), keep_block(3), pool(1)], [grad_done(3), load_w2.wait, load_cot[0].wait]),
            (
                [second(3), up_conv(1), keep_block(2), pool(0)],
                [grad_done(2), load_pre[3].wait, second_done(3)],
            ),
            (
                [second(2), up_conv(0), keep_block(1), pre_grad(3)],
                [grad_done(1), second_done(2), load_w1.wait, load_pre[2].wait],
            ),
            (
                [last(3), second(1), keep_block(0), pre_grad(2)],
                [grad_done(0), second_done(1), load_pre[1].wait, load_feat.wait],
            ),
            (
                [second(0), last(2), pre_grad(1), finish(3)],
                [second_done(0), load_pre[0].wait, store[3].start],
            ),
            ([last(1), pre_grad(0), finish(2)], [store[2].start]),
            ([last(0), finish(1)], [store[1].start]),
            ([finish(0)], [store[0].start]),
        ]
    )
    for copy in store:
        copy.wait()


def halves(field, axis):
    half = field.shape[-1] // 2
    return jnp.concatenate([field[..., :half], field[..., half:]], axis=axis)


def per_device(
    features, conv_first, bias_first, gain_first, conv_second, gain_second, up_weight, cotangent
):
    def cols(lo_f, lo_c):
        parts = [cotangent[:, :, lo_c : lo_c + 5], halves(features[:, :, lo_f : lo_f + 2], 1)]
        return jnp.pad(jnp.concatenate(parts, axis=2), ((0, 0), (0, 0), (0, 1), (0, 0)))

    last_cols, first_cols, w1, w2, wup = lax.optimization_barrier(
        (cols(30, 59), cols(0, 0), conv_first, conv_second, up_weight)
    )
    left, right = shift_pair(last_cols, first_cols, "wa")
    vmem, own = pl.BlockSpec(memory_space=pltpu.VMEM), pl.BlockSpec(memory_space=pltpu.HBM)
    w1t, w2t, wu = pl.pallas_call(
        pack_weights,
        out_shape=[pltpu.HBM((3, 192, 1792), BF16), pltpu.HBM((3, 192, 1792), BF16), pltpu.HBM((192, 1152), BF16)],
        in_specs=[vmem] * 3,
        out_specs=[vmem] * 3,
        compiler_params=pltpu.CompilerParams(vmem_limit_bytes=16 * 1024 * 1024),
        name="pack_weights",
    )(w1, w2, wup)

    def ring(first, last, width):
        gap = jnp.zeros(first.shape[:2] + (width - 2 * first.shape[2], first.shape[3]), BF16)
        return jnp.concatenate([first, gap, last], axis=2)

    cot_side = ring(right[:, :, :5], left[:, :, :5], 16)
    whole = lambda side: jnp.concatenate([side[:, :32, 5:7], side[:, 32:, 5:7]], axis=3)
    feat_side = ring(whole(right), whole(left), 8)

    def rows(field, side, lo, count):
        part = slice(lo, lo + count)
        return jnp.concatenate([field[:, part], side[:, part]], axis=2)

    up, down = rows(features, feat_side, 30, 2), rows(features, feat_side, 0, 2)
    cot_up, cot_down = rows(cotangent, cot_side, 59, 5), rows(cotangent, cot_side, 0, 5)
    up, down, cot_up, cot_down = lax.optimization_barrier((up, down, cot_up, cot_down))
    before, after = shift_pair(up, down, "ha")
    cot_before, cot_after = shift_pair(cot_up, cot_down, "ha")

    bias, gain1, gain2 = (x.reshape(1, 192) for x in (bias_first, gain_first, gain_second))
    ha, wa = lax.axis_index("ha"), lax.axis_index("wa")
    flags = jnp.stack(
        [ha > 0, ha < lax.axis_size("ha") - 1, wa > 0, wa < lax.axis_size("wa") - 1]
    ).astype(jnp.int32)
    pre, pre_strip = pl.pallas_call(
        forward,
        out_shape=[
            pltpu.HBM((4, 34, 32, 192), F32),
            jax.ShapeDtypeStruct((4, DEEP, 16, 192), F32),
        ],
        in_specs=[vmem] * 7,
        out_specs=[own, vmem],
        scratch_shapes=[pltpu.VMEM((36, 32, 640), BF16)] * 4
        + [pltpu.VMEM((DEEP + 2, 16, 640), BF16)] * 4
        + [pltpu.VMEM((5, 8 * (7 + 7 * DEEP), 128), F32), pltpu.VMEM((18, COLS, 192), F32)]
        + [
            pltpu.VMEM((4, 34, 32, 192), F32),
            pltpu.SemaphoreType.DMA((4,)),
        ],
        compiler_params=pltpu.CompilerParams(vmem_limit_bytes=30 * 1024 * 1024),
        cost_estimate=pl.CostEstimate(flops=20_000_000_000, transcendentals=1_000_000, bytes_accessed=12_000_000),
        name="forward_block",
    )(features, feat_side, before, after, conv_first, bias, gain1)
    return pl.pallas_call(
        backward,
        out_shape=jax.ShapeDtypeStruct(features.shape, BF16),
        in_specs=[pl.BlockSpec(memory_space=pltpu.SMEM), own, own, vmem, own] + [vmem] * 3
        + [own, own] + [vmem] * 3,
        out_specs=own,
        scratch_shapes=[pltpu.VMEM((36, 32, 640), BF16)] * 8
        + [pltpu.VMEM((DEEP + 2, 16, 640), BF16)] * 4
        + [pltpu.VMEM((36, 32, 192), F32)] * 4
        + [pltpu.VMEM((36, COLS, 192), F32)] * 2
        + [pltpu.VMEM((34, 32, 192), F32)] * 2
        + [pltpu.VMEM((DEEP, 16, 192), F32)] * 2
        + [pltpu.VMEM((2, 37, WIDE, 384), BF16)] * 2
        + [pltpu.VMEM((32, 32, 192), F32)]
        + [
            pltpu.VMEM((5, 8 * (7 + 7 * DEEP), 128), F32),
            pltpu.VMEM((17, COLS, 192), F32),
            pltpu.VMEM((16 * DEEP, 192), F32),
            pltpu.VMEM((16, 2, 80, 128), F32),
            pltpu.VMEM((COLS, 192), F32),
            pltpu.VMEM((DEEP, 16, 192), F32),
            pltpu.VMEM((4, 32, 32, 192), BF16),
            pltpu.VMEM((4, 34, 32, 192), F32),
            pltpu.VMEM((4, 64, 64, 96), BF16),
            pltpu.VMEM((3, 192, 1792), BF16),
            pltpu.VMEM((3, 192, 1792), BF16),
            pltpu.VMEM((4, 32, 32, 192), BF16),
            pltpu.SemaphoreType.DMA((15,)),
        ],
        compiler_params=pltpu.CompilerParams(vmem_limit_bytes=58 * 1024 * 1024),
        name="backward_block",
    )(
        flags, features, pre, pre_strip, cotangent, cot_side, cot_before, cot_after, w1t, w2t, wu,
        gain1, gain2,
    )


def solution(mesh):
    placed = (P(None, "ha", "wa", None), P(), P(), P(), P(), P(), P(), P(None, "ha", "wa", None))
    return jax.shard_map(
        per_device, mesh=mesh, in_specs=placed, out_specs=P(None, "ha", "wa", None), check_vma=False
    )
```

```python
import jax
import jax.numpy as jnp
from jax import lax
from jax.experimental import pallas as pl
from jax.experimental.pallas import tpu as pltpu
from jax.sharding import PartitionSpec as P

COLS = 40
WIDE = 48
DEEP = 5
LANES = (640, 512, 640)
F32 = jnp.float32
BF16 = jnp.bfloat16


def shift_pair(value_up, value_down, axis):
    count = lax.axis_size(axis)
    up = [(i, (i + 1) % count) for i in range(count - 1)]
    down = [(j, i) for i, j in up]
    return lax.ppermute(value_up, axis, up), lax.ppermute(value_down, axis, down)


def rms_scale(value):
    return lax.rsqrt(jnp.sum(value * value, axis=-1, keepdims=True) * (1.0 / 192) + 1e-06)


def sigmoid(value):
    return 0.5 * jnp.tanh(0.5 * value) + 0.5


def put_row(ref, tail, e, value):
    low, high = value[:, :128], value[:, 128:]
    high = jnp.concatenate([high, high], axis=1)
    lane = lax.broadcasted_iota(jnp.int32, high.shape, 1)
    left = jnp.where(lane < 64, pltpu.roll(high, 1, 0), high)
    after = pltpu.roll(high, COLS - 1, 0)
    before = jnp.maximum(e - 1, 0)
    for n, x in enumerate([pltpu.roll(low, 1, 0), low, pltpu.roll(low, COLS - 1, 0), left]):
        ref[e, :, 128 * n : 128 * n + 128] = x[:32].astype(BF16)
        if tail is not None:
            tail[n, pl.ds(8 * e, 8), :] = x[32:]
    own = after[:32].astype(BF16)
    ref[e, :, 512:576] = own[:, :64]
    ref[before, :, 576:640] = own[:, 64:]
    if tail is not None:
        tail[4, pl.ds(8 * e, 8), 0:64] = after[32:, :64]
        tail[4, pl.ds(8 * before, 8), 64:128] = after[32:, 64:]


def build_strip(dst, tail):
    for r in range(DEEP + 2):
        for n in range(5):
            sides = [tail[n, pl.ds(8 * r + first, 8, stride=8 * DEEP), :] for first in (7, 0)]
            dst[r, :, 128 * n : 128 * n + 128] = jnp.concatenate(sides, axis=0).astype(BF16)


def weight_rows(w_ref, k):
    rows = []
    for p in range(3):
        w = [w_ref[k, p, q] for q in range(3)]
        rows += [w[0][:128], w[1][:128], w[2][:128], w[0][128:], w[1][128:]]
        if p == 0:
            rows += [w[2][128:], w_ref[k, 1, 2, 128:, :]]
        if p == 2:
            rows += [w[2][128:], jnp.zeros((64, 192), BF16)]
    return jnp.concatenate(rows, axis=0)


def pack_adjoint(dst, w_ref):
    for k in range(3):
        base = 0
        for p in range(3):
            w = [w_ref[2 - k, 2 - p, 2 - q] for q in range(3)]
            for q in range(3):
                dst[k, :, base + 128 * q : base + 128 * q + 128] = w[q][:, :128]
            dst[k, :, base + 384 : base + 512] = jnp.concatenate([w[0][:, 128:], w[1][:, 128:]], axis=1)
            if p != 1:
                other = w_ref[2 - k, 1, 0][:, 128:] if p == 0 else jnp.zeros((192, 64), BF16)
                dst[k, :, base + 512 : base + 640] = jnp.concatenate([w[2][:, 128:], other], axis=1)
            base += LANES[p]


def operand(refs, strips, frames, row, rows, strip_row):
    parts = []
    for s in frames:
        for p in range(3):
            lanes = LANES[p]
            piece = refs[s][pl.ds(row + p, rows), :, 0:lanes].reshape(rows * 32, lanes)
            if strips is not None:
                side = strips[s][pl.ds(strip_row + p, 3), :, 0:lanes].reshape(48, lanes)
                piece = jnp.concatenate([piece, side], axis=0)
            parts.append(piece)
    return jnp.concatenate(parts, axis=1)


def conv_dot(lhs, w, axis):
    return lax.dot_general(lhs, w, (((1,), (axis,)), ((), ())), preferred_element_type=F32)


def split(value, b, main, strip, add):
    main[pl.ds(17 * b, 17)] = value[: 17 * 32].reshape(17, 32, 192) + add
    strip[pl.ds(2 * b, 3)] = value[17 * 32 :].reshape(3, 16, 192) + add


def run_steps(steps):
    for jobs, then in steps:

        def step(b, carry):
            for job in jobs:
                job(b)
            return carry

        lax.fori_loop(0, 2, step, 0)
        for job in then:
            job()


def forward(*refs):
    feat, feat_side, before, after, w1, bias, gain1, pre_out, pre_strip = refs[:9]
    act, act_strip = refs[9:13], refs[13:17]
    act_tail, act_rows, pre, sem = refs[17:]
    stores = [pltpu.make_async_copy(pre.at[t], pre_out.at[t], sem.at[t]) for t in range(4)]
    for n in range(4):
        act[n][35, :, 576:640] = jnp.zeros((32, 64), BF16)
    act_tail[:, 35 * 8 :, :] = jnp.zeros((5, 56, 128), F32)

    def activate(t):
        def one(r, x):
            n = x * rms_scale(x) * gain1[...]
            act_rows[r] = n * sigmoid(n)

        def run(b):
            for r in range(2):
                x = jnp.where(b == 0, before[t, r].astype(F32), after[t, r].astype(F32))
                one(r, x)
            for r in range(16):
                i = 16 * b + r
                one(r + 2, jnp.concatenate([feat[t, i].astype(F32), feat_side[t, i].astype(F32)], axis=0))
            for r in range(18):
                put_row(act[t], act_tail, r + 34 * b if r < 2 else r + 16 * b, act_rows[r])

        return run

    def first_conv(t):
        frames = range(max(0, t - 2), t + 1)

        def run(b):
            w = jnp.concatenate([weight_rows(w1, s - t + 2) for s in frames], axis=0)
            lhs = operand(act, act_strip, frames, 17 * b, 17, 2 * b)
            value = conv_dot(lhs, w, 0)
            split(value, b, pre.at[t], pre_strip.at[t], bias[...].reshape(1, 1, 192))

        return run

    done = lambda t: lambda: build_strip(act_strip[t], act_tail)
    run_steps(
        [
            ([activate(0)], [done(0)]),
            ([first_conv(0), activate(1)], [done(1), stores[0].start]),
            ([first_conv(1), activate(2)], [done(2), stores[1].start]),
            ([first_conv(2), activate(3)], [done(3), stores[2].start]),
            ([first_conv(3)], [stores[3].start]),
        ]
    )
    for copy in stores:
        copy.wait()


def backward(*refs):
    flags, feat_in, pre_in, pre_strip, cot_in, cot_side, before, after, w1_in, w2_in = refs[:10]
    wup, gain1, gain2, result = refs[10:14]
    act, grad, grad_strip, block = (refs[14 + 4 * n : 18 + 4 * n] for n in range(4))
    acc_up, acc, acc_strip, pooled = (refs[30 + 2 * n : 32 + 2 * n] for n in range(4))
    acc_last = (refs[38], acc_up[1], acc_up[0], refs[38])
    grad_tail, grad_rows, edges, line, mask, strip_mask, w2t, w1t, wu = refs[39:48]
    feat, pre, cot, w1, w2, out, sem = refs[48:]

    def copies(src, dst, first):
        return [pltpu.make_async_copy(src.at[t], dst.at[t], sem.at[first + t]) for t in range(4)]

    load_cot, load_pre, store = copies(cot_in, cot, 0), copies(pre_in, pre, 4), copies(out, result, 8)
    load_w2 = pltpu.make_async_copy(w2_in, w2, sem.at[12])
    load_w1 = pltpu.make_async_copy(w1_in, w1, sem.at[13])
    load_feat = pltpu.make_async_copy(feat_in, feat, sem.at[14])
    for copy in (load_cot[3], load_w2, load_cot[2], load_cot[1], load_cot[0], load_pre[3], load_w1):
        copy.start()
    for copy in (load_pre[2], load_pre[1], load_feat, load_pre[0]):
        copy.start()

    for n in range(4):
        act[n][35, :, 576:640] = jnp.zeros((32, 64), BF16)
        grad[n][35, :, 576:640] = jnp.zeros((32, 64), BF16)
    grad_tail[:, 35 * 8 :, :] = jnp.zeros((5, 56, 128), F32)
    line[...] = jnp.zeros_like(line)
    s = lax.broadcasted_iota(jnp.int32, mask.shape, 0)
    good = (s < 32) | ((s < 34) & (flags[3] > 0)) | ((s >= 38) & (flags[2] > 0))
    mask[...] = jnp.where(good, 1.0, 0.0)
    r, s = (lax.broadcasted_iota(jnp.int32, strip_mask.shape, n) for n in range(2))
    o = DEEP * lax.rem(s, 8) + r
    good = jnp.where(s < 8, flags[2], flags[3]) > 0
    good &= ((o > 0) | (flags[0] > 0)) & ((o < 33) | (flags[1] > 0))
    strip_mask[...] = jnp.where(good, 1.0, 0.0)
    for p in range(3):
        for q in range(3):
            tap = 128 * (3 * p + q)
            wu[:, tap : tap + 96] = wup[2 - p, 2 - q]
            wu[:, tap + 96 : tap + 128] = jnp.zeros((192, 32), BF16)

    def edge(value, b, r, first, last):
        if r in first:
            return value * jnp.where((b == 0) & (flags[0] == 0), 0.0, 1.0)
        if r in last:
            return value * jnp.where((b == 1) & (flags[1] == 0), 0.0, 1.0)
        return value

    def pool(t):
        dst = pooled[t % 2]

        def own(y):
            return jnp.concatenate([cot[t, y], cot_side[t, y]], axis=0).astype(F32)

        def one(e, rows, slot):
            for m in range(2):
                line[slot, m, :, 0:96] = rows[m] + rows[m + 1]
                even = line[slot, m, pl.ds(0, 40, stride=2), :]
                odd = line[slot, m, pl.ds(1, 40, stride=2), :]
                dst[m, e, :COLS, 0:128] = (pltpu.roll(odd, 1, 0) + even).astype(BF16)
                dst[m, e, :COLS, 128:256] = (even + odd).astype(BF16)
                dst[m, e, :COLS, 256:384] = (odd + pltpu.roll(even, 39, 0)).astype(BF16)

        def run(b):
            top = [before[t, r].astype(F32) for r in range(5)] + [own(0), own(1)]
            low = [own(63)] + [after[t, r].astype(F32) for r in range(5)]
            low.append(low[-1])
            ends = [jnp.where(b == 0, x, y) for x, y in zip(top, low)]
            for r in range(3):
                one(34 * b + r, ends[2 * r : 2 * r + 3], r)
            for r in range(16):
                e = jnp.minimum(3 + 16 * b + r, 33)
                one(e, [own(2 * e - 5 + m) for m in range(3)], 3 + r % 13)

        return run

    def keep_block(t):
        def run(b):
            for r in range(18):
                e = 18 * b + r
                value = edge(acc_up[t % 2][e] * mask[...], b, r, (0, 1), (16, 17))
                put_row(grad[t], grad_tail, e, value)
                block[t][e] = value[:32]

        return run

    def norm_back(v, gain, top):
        scale = rms_scale(v)
        n = v * scale * gain
        s = sigmoid(n)
        u = gain * (top * (s * (1.0 + n * (1.0 - s))))
        mean = jnp.sum(v * u, axis=-1, keepdims=True) * (1.0 / 192)
        return scale * u - v * (scale * scale * scale * mean)

    def strip_grad(t):
        g = norm_back(pre_strip[t], gain2[...].reshape(1, 1, 192), acc_strip[t % 2][...])
        g = g * strip_mask[...]
        for r in range(DEEP):
            edges[16 * r : 16 * r + 16, :] = g[r]

    def pre_grad(t):
        spot = lax.broadcasted_iota(jnp.int32, (8, 192), 0)

        def run(b):
            for r in range(17):
                o = 17 * b + r
                g = norm_back(pre[t, o], gain2[...], acc[t % 2][o])
                at = 16 * lax.rem(o, DEEP) + lax.div(o, DEEP)
                left, right = edges[pl.ds(at, 1), :], edges[pl.ds(at + 8, 1), :]
                grad_rows[r, :32] = edge(g, b, r, (0,), (16,))
                grad_rows[r, 32:] = jnp.where(spot == 0, right, jnp.where(spot == 7, left, 0.0))
            for r in range(17):
                put_row(act[t], None, 17 * b + r, grad_rows[r])

        return run

    def finish(t):
        def run(b):
            for r in range(16):
                i = 16 * b + r
                g = norm_back(feat[t, i].astype(F32), gain1[...], acc_last[t][i, :32])
                out[t, i] = (block[t][i + 2] + g).astype(BF16)

        return run

    def transposed(lhs, w, frames):
        return conv_dot(lhs, jnp.concatenate([w[s - frames[0]] for s in frames], axis=1), 1)

    def second(t):
        frames = range(t, min(4, t + 3))

        def run(b):
            value = transposed(operand(grad, grad_strip, frames, 17 * b, 17, 2 * b), w2t, frames)
            split(value, b, acc[t % 2], acc_strip[t % 2], 0.0)

        return run

    def last(t):
        frames = range(t, min(4, t + 3))

        def run(b):
            value = transposed(operand(act, None, frames, 16 * b, 16, 0), w1t, frames)
            acc_last[t][pl.ds(16 * b, 16), :32] = value.reshape(16, 32, 192)

        return run

    def up_conv(t):
        src = pooled[t % 2]

        def run(b):
            parts = [src[0, pl.ds(18 * b, 18)], src[1, pl.ds(18 * b, 18)], src[0, pl.ds(18 * b + 1, 18)]]
            lhs = jnp.concatenate([x.reshape(18 * WIDE, 384) for x in parts], axis=1)
            value = conv_dot(lhs, wu[...], 1)
            acc_up[t % 2][pl.ds(18 * b, 18)] = value.reshape(18, WIDE, 192)[:, :COLS]

        return run

    grad_done = lambda t: lambda: build_strip(grad_strip[t], grad_tail)
    second_done = lambda t: lambda: strip_grad(t)
    pack2, pack1 = lambda: pack_adjoint(w2t, w2), lambda: pack_adjoint(w1t, w1)
    load_cot[3].wait()
    run_steps(
        [
            ([pool(3)], [load_cot[2].wait]),
            ([up_conv(3), pool(2)], [load_cot[1].wait]),
            ([up_conv(2), keep_block(3), pool(1)], [grad_done(3), load_w2.wait, pack2, load_cot[0].wait]),
            (
                [second(3), up_conv(1), keep_block(2), pool(0)],
                [grad_done(2), load_pre[3].wait, second_done(3)],
            ),
            (
                [second(2), up_conv(0), keep_block(1), pre_grad(3)],
                [grad_done(1), second_done(2), load_w1.wait, pack1, load_pre[2].wait],
            ),
            (
                [last(3), second(1), keep_block(0), pre_grad(2)],
                [grad_done(0), second_done(1), load_pre[1].wait, load_feat.wait],
            ),
            (
                [second(0), last(2), pre_grad(1), finish(3)],
                [second_done(0), load_pre[0].wait, store[3].start],
            ),
            ([last(1), pre_grad(0), finish(2)], [store[2].start]),
            ([last(0), finish(1)], [store[1].start]),
            ([finish(0)], [store[0].start]),
        ]
    )
    for copy in store:
        copy.wait()


def halves(field, axis):
    half = field.shape[-1] // 2
    return jnp.concatenate([field[..., :half], field[..., half:]], axis=axis)


def per_device(
    features, conv_first, bias_first, gain_first, conv_second, gain_second, up_weight, cotangent
):
    def cols(lo_f, lo_c):
        parts = [cotangent[:, :, lo_c : lo_c + 5], halves(features[:, :, lo_f : lo_f + 2], 1)]
        return jnp.pad(jnp.concatenate(parts, axis=2), ((0, 0), (0, 0), (0, 1), (0, 0)))

    left, right = shift_pair(cols(30, 59), cols(0, 0), "wa")

    def ring(first, last, width):
        gap = jnp.zeros(first.shape[:2] + (width - 2 * first.shape[2], first.shape[3]), BF16)
        return jnp.concatenate([first, gap, last], axis=2)

    cot_side = ring(right[:, :, :5], left[:, :, :5], 16)
    whole = lambda side: jnp.concatenate([side[:, :32, 5:7], side[:, 32:, 5:7]], axis=3)
    feat_side = ring(whole(right), whole(left), 8)

    def rows(field, side, lo, count):
        part = slice(lo, lo + count)
        return jnp.concatenate([field[:, part], side[:, part]], axis=2)

    up, down = rows(features, feat_side, 30, 2), rows(features, feat_side, 0, 2)
    cot_up, cot_down = rows(cotangent, cot_side, 59, 5), rows(cotangent, cot_side, 0, 5)
    up, down, cot_up, cot_down = lax.optimization_barrier((up, down, cot_up, cot_down))
    before, after = shift_pair(up, down, "ha")
    cot_before, cot_after = shift_pair(cot_up, cot_down, "ha")

    bias, gain1, gain2 = (x.reshape(1, 192) for x in (bias_first, gain_first, gain_second))
    ha, wa = lax.axis_index("ha"), lax.axis_index("wa")
    flags = jnp.stack(
        [ha > 0, ha < lax.axis_size("ha") - 1, wa > 0, wa < lax.axis_size("wa") - 1]
    ).astype(jnp.int32)
    vmem, own = pl.BlockSpec(memory_space=pltpu.VMEM), pl.BlockSpec(memory_space=pltpu.HBM)
    pre, pre_strip = pl.pallas_call(
        forward,
        out_shape=[
            pltpu.HBM((4, 34, 32, 192), F32),
            pltpu.HBM((4, DEEP, 16, 192), F32),
        ],
        in_specs=[vmem] * 7,
        out_specs=[own, vmem],
        scratch_shapes=[pltpu.VMEM((36, 32, 640), BF16)] * 4
        + [pltpu.VMEM((DEEP + 2, 16, 640), BF16)] * 4
        + [pltpu.VMEM((5, 8 * (7 + 7 * DEEP), 128), F32), pltpu.VMEM((18, COLS, 192), F32)]
        + [
            pltpu.VMEM((4, 34, 32, 192), F32),
            pltpu.SemaphoreType.DMA((4,)),
        ],
        compiler_params=pltpu.CompilerParams(vmem_limit_bytes=30 * 1024 * 1024),
        cost_estimate=pl.CostEstimate(flops=20_000_000_000, transcendentals=1_000_000, bytes_accessed=12_000_000),
        name="forward_block",
    )(features, feat_side, before, after, conv_first, bias, gain1)
    return pl.pallas_call(
        backward,
        out_shape=jax.ShapeDtypeStruct(features.shape, BF16),
        in_specs=[pl.BlockSpec(memory_space=pltpu.SMEM), own, own, vmem, own] + [vmem] * 3
        + [own, own] + [vmem] * 3,
        out_specs=own,
        scratch_shapes=[pltpu.VMEM((36, 32, 640), BF16)] * 8
        + [pltpu.VMEM((DEEP + 2, 16, 640), BF16)] * 4
        + [pltpu.VMEM((36, 32, 192), F32)] * 4
        + [pltpu.VMEM((36, COLS, 192), F32)] * 2
        + [pltpu.VMEM((34, 32, 192), F32)] * 2
        + [pltpu.VMEM((DEEP, 16, 192), F32)] * 2
        + [pltpu.VMEM((2, 37, WIDE, 384), BF16)] * 2
        + [pltpu.VMEM((32, 32, 192), F32)]
        + [
            pltpu.VMEM((5, 8 * (7 + 7 * DEEP), 128), F32),
            pltpu.VMEM((17, COLS, 192), F32),
            pltpu.VMEM((16 * DEEP, 192), F32),
            pltpu.VMEM((16, 2, 80, 128), F32),
            pltpu.VMEM((COLS, 192), F32),
            pltpu.VMEM((DEEP, 16, 192), F32),
            pltpu.VMEM((3, 192, 1792), BF16),
            pltpu.VMEM((3, 192, 1792), BF16),
            pltpu.VMEM((192, 1152), BF16),
            pltpu.VMEM((4, 32, 32, 192), BF16),
            pltpu.VMEM((4, 34, 32, 192), F32),
            pltpu.VMEM((4, 64, 64, 96), BF16),
            pltpu.VMEM((3, 3, 3, 192, 192), BF16),
            pltpu.VMEM((3, 3, 3, 192, 192), BF16),
            pltpu.VMEM((4, 32, 32, 192), BF16),
            pltpu.SemaphoreType.DMA((15,)),
        ],
        compiler_params=pltpu.CompilerParams(vmem_limit_bytes=58 * 1024 * 1024),
        name="backward_block",
    )(
        flags, features, pre, pre_strip, cotangent, cot_side, cot_before, cot_after, conv_first,
        conv_second, up_weight, gain1, gain2,
    )


def solution(mesh):
    placed = (P(None, "ha", "wa", None), P(), P(), P(), P(), P(), P(), P(None, "ha", "wa", None))
    return jax.shard_map(
        per_device, mesh=mesh, in_specs=placed, out_specs=P(None, "ha", "wa", None), check_vma=False
    )
```

```python
import jax
import jax.numpy as jnp
from jax import lax
from jax.experimental import pallas as pl
from jax.experimental.pallas import tpu as pltpu
from jax.sharding import PartitionSpec as P

COLS = 40
WIDE = 48
DEEP = 5
LANES = (640, 512, 640)
F32 = jnp.float32
BF16 = jnp.bfloat16


def shift_pair(value_up, value_down, axis):
    count = lax.axis_size(axis)
    up = [(i, (i + 1) % count) for i in range(count - 1)]
    down = [(j, i) for i, j in up]
    return lax.ppermute(value_up, axis, up), lax.ppermute(value_down, axis, down)


def rms_scale(value):
    return lax.rsqrt(jnp.sum(value * value, axis=-1, keepdims=True) * (1.0 / 192) + 1e-06)


def sigmoid(value):
    return 0.5 * jnp.tanh(0.5 * value) + 0.5


def put_row(ref, tail, e, value):
    low, high = value[:, :128], value[:, 128:]
    high = jnp.concatenate([high, high], axis=1)
    lane = lax.broadcasted_iota(jnp.int32, high.shape, 1)
    left = jnp.where(lane < 64, pltpu.roll(high, 1, 0), high)
    after = pltpu.roll(high, COLS - 1, 0)
    before = jnp.maximum(e - 1, 0)
    for n, x in enumerate([pltpu.roll(low, 1, 0), low, pltpu.roll(low, COLS - 1, 0), left]):
        ref[e, :, 128 * n : 128 * n + 128] = x[:32].astype(BF16)
        if tail is not None:
            tail[n, pl.ds(8 * e, 8), :] = x[32:]
    own = after[:32].astype(BF16)
    ref[e, :, 512:576] = own[:, :64]
    ref[before, :, 576:640] = own[:, 64:]
    if tail is not None:
        tail[4, pl.ds(8 * e, 8), 0:64] = after[32:, :64]
        tail[4, pl.ds(8 * before, 8), 64:128] = after[32:, 64:]


def build_strip(dst, tail):
    for r in range(DEEP + 2):
        for n in range(5):
            sides = [tail[n, pl.ds(8 * r + first, 8, stride=8 * DEEP), :] for first in (7, 0)]
            dst[r, :, 128 * n : 128 * n + 128] = jnp.concatenate(sides, axis=0).astype(BF16)


def weight_rows(w_ref, k):
    rows = []
    for p in range(3):
        w = [w_ref[k, p, q] for q in range(3)]
        rows += [w[0][:128], w[1][:128], w[2][:128], w[0][128:], w[1][128:]]
        if p == 0:
            rows += [w[2][128:], w_ref[k, 1, 2, 128:, :]]
        if p == 2:
            rows += [w[2][128:], jnp.zeros((64, 192), BF16)]
    return jnp.concatenate(rows, axis=0)


def pack_adjoint(dst, w_ref):
    for k in range(3):
        base = 0
        for p in range(3):
            w = [w_ref[2 - k, 2 - p, 2 - q] for q in range(3)]
            for q in range(3):
                dst[k, :, base + 128 * q : base + 128 * q + 128] = w[q][:, :128]
            dst[k, :, base + 384 : base + 512] = jnp.concatenate([w[0][:, 128:], w[1][:, 128:]], axis=1)
            if p != 1:
                other = w_ref[2 - k, 1, 0][:, 128:] if p == 0 else jnp.zeros((192, 64), BF16)
                dst[k, :, base + 512 : base + 640] = jnp.concatenate([w[2][:, 128:], other], axis=1)
            base += LANES[p]


def operand(refs, strips, frames, row, rows, strip_row):
    parts = []
    for s in frames:
        for p in range(3):
            lanes = LANES[p]
            piece = refs[s][pl.ds(row + p, rows), :, 0:lanes].reshape(rows * 32, lanes)
            if strips is not None:
                side = strips[s][pl.ds(strip_row + p, 3), :, 0:lanes].reshape(48, lanes)
                piece = jnp.concatenate([piece, side], axis=0)
            parts.append(piece)
    return jnp.concatenate(parts, axis=1)


def conv_dot(lhs, w, axis):
    return lax.dot_general(lhs, w, (((1,), (axis,)), ((), ())), preferred_element_type=F32)


def split(value, b, main, strip, add):
    main[pl.ds(17 * b, 17)] = value[: 17 * 32].reshape(17, 32, 192) + add
    strip[pl.ds(2 * b, 3)] = value[17 * 32 :].reshape(3, 16, 192) + add


def run_steps(steps):
    for jobs, then in steps:

        def step(b, carry):
            for job in jobs:
                job(b)
            return carry

        lax.fori_loop(0, 2, step, 0)
        for job in then:
            job()


def forward(*refs):
    feat, feat_side, before, after, w1_in, bias, gain1, pre_out, pre_strip = refs[:9]
    act, act_strip = refs[9:13], refs[13:17]
    act_tail, act_rows, pre, w1, sem = refs[17:]
    load_w1 = pltpu.make_async_copy(w1_in, w1, sem.at[4])
    load_w1.start()
    stores = [pltpu.make_async_copy(pre.at[t], pre_out.at[t], sem.at[t]) for t in range(4)]
    for n in range(4):
        act[n][35, :, 576:640] = jnp.zeros((32, 64), BF16)
    act_tail[:, 35 * 8 :, :] = jnp.zeros((5, 56, 128), F32)

    def activate(t):
        def one(r, x):
            n = x * rms_scale(x) * gain1[...]
            act_rows[r] = n * sigmoid(n)

        def run(b):
            for r in range(2):
                x = jnp.where(b == 0, before[t, r].astype(F32), after[t, r].astype(F32))
                one(r, x)
            for r in range(16):
                i = 16 * b + r
                one(r + 2, jnp.concatenate([feat[t, i].astype(F32), feat_side[t, i].astype(F32)], axis=0))
            for r in range(18):
                put_row(act[t], act_tail, r + 34 * b if r < 2 else r + 16 * b, act_rows[r])

        return run

    def first_conv(t):
        frames = range(max(0, t - 2), t + 1)

        def run(b):
            w = jnp.concatenate([weight_rows(w1, s - t + 2) for s in frames], axis=0)
            lhs = operand(act, act_strip, frames, 17 * b, 17, 2 * b)
            value = conv_dot(lhs, w, 0)
            split(value, b, pre.at[t], pre_strip.at[t], bias[...].reshape(1, 1, 192))

        return run

    done = lambda t: lambda: build_strip(act_strip[t], act_tail)
    run_steps(
        [
            ([activate(0)], [done(0), load_w1.wait]),
            ([first_conv(0), activate(1)], [done(1), stores[0].start]),
            ([first_conv(1), activate(2)], [done(2), stores[1].start]),
            ([first_conv(2), activate(3)], [done(3), stores[2].start]),
            ([first_conv(3)], [stores[3].start]),
        ]
    )
    for copy in stores:
        copy.wait()


def backward(*refs):
    flags, feat_in, pre_in, pre_strip, cot_in, cot_side, before, after, w1_in, w2_in = refs[:10]
    wup, gain1, gain2, result = refs[10:14]
    act, grad, grad_strip, block = (refs[14 + 4 * n : 18 + 4 * n] for n in range(4))
    acc_up, acc, acc_strip, pooled = (refs[30 + 2 * n : 32 + 2 * n] for n in range(4))
    acc_last = (refs[38], acc_up[1], acc_up[0], refs[38])
    grad_tail, grad_rows, edges, line, mask, strip_mask, w2t, w1t, wu = refs[39:48]
    feat, pre, cot, w1, w2, out, sem = refs[48:]

    def copies(src, dst, first):
        return [pltpu.make_async_copy(src.at[t], dst.at[t], sem.at[first + t]) for t in range(4)]

    load_cot, load_pre, store = copies(cot_in, cot, 0), copies(pre_in, pre, 4), copies(out, result, 8)
    load_w2 = pltpu.make_async_copy(w2_in, w2, sem.at[12])
    load_w1 = pltpu.make_async_copy(w1_in, w1, sem.at[13])
    load_feat = pltpu.make_async_copy(feat_in, feat, sem.at[14])
    for copy in (load_cot[3], load_w2, load_cot[2], load_cot[1], load_cot[0], load_pre[3], load_w1):
        copy.start()
    for copy in (load_pre[2], load_pre[1], load_feat, load_pre[0]):
        copy.start()

    for n in range(4):
        act[n][35, :, 576:640] = jnp.zeros((32, 64), BF16)
        grad[n][35, :, 576:640] = jnp.zeros((32, 64), BF16)
    grad_tail[:, 35 * 8 :, :] = jnp.zeros((5, 56, 128), F32)
    line[...] = jnp.zeros_like(line)
    s = lax.broadcasted_iota(jnp.int32, mask.shape, 0)
    good = (s < 32) | ((s < 34) & (flags[3] > 0)) | ((s >= 38) & (flags[2] > 0))
    mask[...] = jnp.where(good, 1.0, 0.0)
    r, s = (lax.broadcasted_iota(jnp.int32, strip_mask.shape, n) for n in range(2))
    o = DEEP * lax.rem(s, 8) + r
    good = jnp.where(s < 8, flags[2], flags[3]) > 0
    good &= ((o > 0) | (flags[0] > 0)) & ((o < 33) | (flags[1] > 0))
    strip_mask[...] = jnp.where(good, 1.0, 0.0)
    for p in range(3):
        for q in range(3):
            tap = 128 * (3 * p + q)
            wu[:, tap : tap + 96] = wup[2 - p, 2 - q]
            wu[:, tap + 96 : tap + 128] = jnp.zeros((192, 32), BF16)

    def edge(value, b, r, first, last):
        if r in first:
            return value * jnp.where((b == 0) & (flags[0] == 0), 0.0, 1.0)
        if r in last:
            return value * jnp.where((b == 1) & (flags[1] == 0), 0.0, 1.0)
        return value

    def pool(t):
        dst = pooled[t % 2]

        def own(y):
            return jnp.concatenate([cot[t, y], cot_side[t, y]], axis=0).astype(F32)

        def one(e, rows, slot):
            for m in range(2):
                line[slot, m, :, 0:96] = rows[m] + rows[m + 1]
                even = line[slot, m, pl.ds(0, 40, stride=2), :]
                odd = line[slot, m, pl.ds(1, 40, stride=2), :]
                dst[m, e, :COLS, 0:128] = (pltpu.roll(odd, 1, 0) + even).astype(BF16)
                dst[m, e, :COLS, 128:256] = (even + odd).astype(BF16)
                dst[m, e, :COLS, 256:384] = (odd + pltpu.roll(even, 39, 0)).astype(BF16)

        def run(b):
            top = [before[t, r].astype(F32) for r in range(5)] + [own(0), own(1)]
            low = [own(63)] + [after[t, r].astype(F32) for r in range(5)]
            low.append(low[-1])
            ends = [jnp.where(b == 0, x, y) for x, y in zip(top, low)]
            for r in range(3):
                one(34 * b + r, ends[2 * r : 2 * r + 3], r)
            for r in range(16):
                e = jnp.minimum(3 + 16 * b + r, 33)
                one(e, [own(2 * e - 5 + m) for m in range(3)], 3 + r % 13)

        return run

    def keep_block(t):
        def run(b):
            for r in range(18):
                e = 18 * b + r
                value = edge(acc_up[t % 2][e] * mask[...], b, r, (0, 1), (16, 17))
                put_row(grad[t], grad_tail, e, value)
                block[t][e] = value[:32]

        return run

    def norm_back(v, gain, top):
        scale = rms_scale(v)
        n = v * scale * gain
        s = sigmoid(n)
        u = gain * (top * (s * (1.0 + n * (1.0 - s))))
        mean = jnp.sum(v * u, axis=-1, keepdims=True) * (1.0 / 192)
        return scale * u - v * (scale * scale * scale * mean)

    def strip_grad(t):
        g = norm_back(pre_strip[t], gain2[...].reshape(1, 1, 192), acc_strip[t % 2][...])
        g = g * strip_mask[...]
        for r in range(DEEP):
            edges[16 * r : 16 * r + 16, :] = g[r]

    def pre_grad(t):
        spot = lax.broadcasted_iota(jnp.int32, (8, 192), 0)

        def run(b):
            for r in range(17):
                o = 17 * b + r
                g = norm_back(pre[t, o], gain2[...], acc[t % 2][o])
                at = 16 * lax.rem(o, DEEP) + lax.div(o, DEEP)
                left, right = edges[pl.ds(at, 1), :], edges[pl.ds(at + 8, 1), :]
                grad_rows[r, :32] = edge(g, b, r, (0,), (16,))
                grad_rows[r, 32:] = jnp.where(spot == 0, right, jnp.where(spot == 7, left, 0.0))
            for r in range(17):
                put_row(act[t], None, 17 * b + r, grad_rows[r])

        return run

    def finish(t):
        def run(b):
            for r in range(16):
                i = 16 * b + r
                g = norm_back(feat[t, i].astype(F32), gain1[...], acc_last[t][i, :32])
                out[t, i] = (block[t][i + 2] + g).astype(BF16)

        return run

    def transposed(lhs, w, frames):
        return conv_dot(lhs, jnp.concatenate([w[s - frames[0]] for s in frames], axis=1), 1)

    def second(t):
        frames = range(t, min(4, t + 3))

        def run(b):
            value = transposed(operand(grad, grad_strip, frames, 17 * b, 17, 2 * b), w2t, frames)
            split(value, b, acc[t % 2], acc_strip[t % 2], 0.0)

        return run

    def last(t):
        frames = range(t, min(4, t + 3))

        def run(b):
            value = transposed(operand(act, None, frames, 16 * b, 16, 0), w1t, frames)
            acc_last[t][pl.ds(16 * b, 16), :32] = value.reshape(16, 32, 192)

        return run

    def up_conv(t):
        src = pooled[t % 2]

        def run(b):
            parts = [src[0, pl.ds(18 * b, 18)], src[1, pl.ds(18 * b, 18)], src[0, pl.ds(18 * b + 1, 18)]]
            lhs = jnp.concatenate([x.reshape(18 * WIDE, 384) for x in parts], axis=1)
            value = conv_dot(lhs, wu[...], 1)
            acc_up[t % 2][pl.ds(18 * b, 18)] = value.reshape(18, WIDE, 192)[:, :COLS]

        return run

    grad_done = lambda t: lambda: build_strip(grad_strip[t], grad_tail)
    second_done = lambda t: lambda: strip_grad(t)
    pack2, pack1 = lambda: pack_adjoint(w2t, w2), lambda: pack_adjoint(w1t, w1)
    load_cot[3].wait()
    run_steps(
        [
            ([pool(3)], [load_cot[2].wait]),
            ([up_conv(3), pool(2)], [load_cot[1].wait]),
            ([up_conv(2), keep_block(3), pool(1)], [grad_done(3), load_w2.wait, pack2, load_cot[0].wait]),
            (
                [second(3), up_conv(1), keep_block(2), pool(0)],
                [grad_done(2), load_pre[3].wait, second_done(3)],
            ),
            (
                [second(2), up_conv(0), keep_block(1), pre_grad(3)],
                [grad_done(1), second_done(2), load_w1.wait, pack1, load_pre[2].wait],
            ),
            (
                [last(3), second(1), keep_block(0), pre_grad(2)],
                [grad_done(0), second_done(1), load_pre[1].wait, load_feat.wait],
            ),
            (
                [second(0), last(2), pre_grad(1), finish(3)],
                [second_done(0), load_pre[0].wait, store[3].start],
            ),
            ([last(1), pre_grad(0), finish(2)], [store[2].start]),
            ([last(0), finish(1)], [store[1].start]),
            ([finish(0)], [store[0].start]),
        ]
    )
    for copy in store:
        copy.wait()


def halves(field, axis):
    half = field.shape[-1] // 2
    return jnp.concatenate([field[..., :half], field[..., half:]], axis=axis)


def per_device(
    features, conv_first, bias_first, gain_first, conv_second, gain_second, up_weight, cotangent
):
    def cols(lo_f, lo_c):
        parts = [cotangent[:, :, lo_c : lo_c + 5], halves(features[:, :, lo_f : lo_f + 2], 1)]
        return jnp.pad(jnp.concatenate(parts, axis=2), ((0, 0), (0, 0), (0, 1), (0, 0)))

    left, right = shift_pair(cols(30, 59), cols(0, 0), "wa")

    def ring(first, last, width):
        gap = jnp.zeros(first.shape[:2] + (width - 2 * first.shape[2], first.shape[3]), BF16)
        return jnp.concatenate([first, gap, last], axis=2)

    cot_side = ring(right[:, :, :5], left[:, :, :5], 16)
    whole = lambda side: jnp.concatenate([side[:, :32, 5:7], side[:, 32:, 5:7]], axis=3)
    feat_side = ring(whole(right), whole(left), 8)

    def rows(field, side, lo, count):
        part = slice(lo, lo + count)
        return jnp.concatenate([field[:, part], side[:, part]], axis=2)

    up, down = rows(features, feat_side, 30, 2), rows(features, feat_side, 0, 2)
    cot_up, cot_down = rows(cotangent, cot_side, 59, 5), rows(cotangent, cot_side, 0, 5)
    up, down, cot_up, cot_down = lax.optimization_barrier((up, down, cot_up, cot_down))
    before, after = shift_pair(up, down, "ha")
    cot_before, cot_after = shift_pair(cot_up, cot_down, "ha")

    bias, gain1, gain2 = (x.reshape(1, 192) for x in (bias_first, gain_first, gain_second))
    ha, wa = lax.axis_index("ha"), lax.axis_index("wa")
    flags = jnp.stack(
        [ha > 0, ha < lax.axis_size("ha") - 1, wa > 0, wa < lax.axis_size("wa") - 1]
    ).astype(jnp.int32)
    vmem, own = pl.BlockSpec(memory_space=pltpu.VMEM), pl.BlockSpec(memory_space=pltpu.HBM)
    pre, pre_strip = pl.pallas_call(
        forward,
        out_shape=[
            pltpu.HBM((4, 34, 32, 192), F32),
            pltpu.HBM((4, DEEP, 16, 192), F32),
        ],
        in_specs=[vmem] * 4 + [own] + [vmem] * 2,
        out_specs=[own, vmem],
        scratch_shapes=[pltpu.VMEM((36, 32, 640), BF16)] * 4
        + [pltpu.VMEM((DEEP + 2, 16, 640), BF16)] * 4
        + [pltpu.VMEM((5, 8 * (7 + 7 * DEEP), 128), F32), pltpu.VMEM((18, COLS, 192), F32)]
        + [
            pltpu.VMEM((4, 34, 32, 192), F32),
            pltpu.VMEM((3, 3, 3, 192, 192), BF16),
            pltpu.SemaphoreType.DMA((5,)),
        ],
        compiler_params=pltpu.CompilerParams(vmem_limit_bytes=34 * 1024 * 1024),
        cost_estimate=pl.CostEstimate(flops=20_000_000_000, transcendentals=1_000_000, bytes_accessed=12_000_000),
        name="forward_block",
    )(features, feat_side, before, after, conv_first, bias, gain1)
    return pl.pallas_call(
        backward,
        out_shape=jax.ShapeDtypeStruct(features.shape, BF16),
        in_specs=[pl.BlockSpec(memory_space=pltpu.SMEM), own, own, vmem, own] + [vmem] * 3
        + [own, own] + [vmem] * 3,
        out_specs=own,
        scratch_shapes=[pltpu.VMEM((36, 32, 640), BF16)] * 8
        + [pltpu.VMEM((DEEP + 2, 16, 640), BF16)] * 4
        + [pltpu.VMEM((36, 32, 192), F32)] * 4
        + [pltpu.VMEM((36, COLS, 192), F32)] * 2
        + [pltpu.VMEM((34, 32, 192), F32)] * 2
        + [pltpu.VMEM((DEEP, 16, 192), F32)] * 2
        + [pltpu.VMEM((2, 37, WIDE, 384), BF16)] * 2
        + [pltpu.VMEM((32, 32, 192), F32)]
        + [
            pltpu.VMEM((5, 8 * (7 + 7 * DEEP), 128), F32),
            pltpu.VMEM((17, COLS, 192), F32),
            pltpu.VMEM((16 * DEEP, 192), F32),
            pltpu.VMEM((16, 2, 80, 128), F32),
            pltpu.VMEM((COLS, 192), F32),
            pltpu.VMEM((DEEP, 16, 192), F32),
            pltpu.VMEM((3, 192, 1792), BF16),
            pltpu.VMEM((3, 192, 1792), BF16),
            pltpu.VMEM((192, 1152), BF16),
            pltpu.VMEM((4, 32, 32, 192), BF16),
            pltpu.VMEM((4, 34, 32, 192), F32),
            pltpu.VMEM((4, 64, 64, 96), BF16),
            pltpu.VMEM((3, 3, 3, 192, 192), BF16),
            pltpu.VMEM((3, 3, 3, 192, 192), BF16),
            pltpu.VMEM((4, 32, 32, 192), BF16),
            pltpu.SemaphoreType.DMA((15,)),
        ],
        compiler_params=pltpu.CompilerParams(vmem_limit_bytes=58 * 1024 * 1024),
        name="backward_block",
    )(
        flags, features, pre, pre_strip, cotangent, cot_side, cot_before, cot_after, conv_first,
        conv_second, up_weight, gain1, gain2,
    )


def solution(mesh):
    placed = (P(None, "ha", "wa", None), P(), P(), P(), P(), P(), P(), P(None, "ha", "wa", None))
    return jax.shard_map(
        per_device, mesh=mesh, in_specs=placed, out_specs=P(None, "ha", "wa", None), check_vma=False
    )
```
